128 devices in a mesh: dp: 4 (over z), cls: 32 (over y, x, core).
Axes of the slice: x: 4, y: 4, z: 4, core: 2. Of those that a mesh axis runs over, the one named last changes fastest.
Arguments:
- embeddings: bfloat16 [8192, 512], P(('dp', 'cls')), may hold values from -6 to 6
- labels: int32 [8192], P('dp'), may hold values from 0 to 65535
- centres: bfloat16 [131072, 512], P('cls'), may hold values from -0.25 to 0.25
- momentum: float32 [131072, 512], P('cls'), may hold values from -3 to 3
- sample_home: int32 [65536, 1], P('cls'), may hold values from 0 to 31; in each aligned block of 2048 rows (0 to 2047, 2048 to 4095, ...) at most 128 rows name the same one
- sample_row: int32 [65536], P('cls'), may hold values from 0 to 4095
Outputs:
- emb_grad: float32 [8192, 512], P(('dp', 'cls'))
- momentum_new: float32 [131072, 512], P('cls')
- centres_new: bfloat16 [131072, 512], P('cls')
The draws below stay inside these ranges and needn't reach their ends.
Inputs may be any that keep to these rules, and one draw needn't show every extreme that they name: Among the 2048 sampled columns of one class tile (aligned blocks of sample_home), at most 128 name the same home shard, and in every draw some home shard supplies exactly 128 columns of some tile.
All inputs are finite; a program needn't handle non-finite values.
Results may differ from the reference program's by a relative error of at most 0.014.
Values may be sent and summed in bfloat16 or wider, within the bound.
A program may use at most 128 MiB of HBM per device.

```python
import math
import jax
import jax.numpy as jnp
import numpy as np
from jax import lax

EMBEDDING_WIDTH = 512
CLS_DEV = 4096
SAMP_DEV = 2048
ROW_DEV = 64
CAP = 128
CLASSES = 131072
SAMPLED = 65536
BATCH = 8192
N_DP = 4
N_CLS = 32


def with_ends(drawn, stream_key, smallest, largest):
    longest = drawn.shape.index(max(drawn.shape))
    spots = []
    for shift in (0, 1):
        where = [jax.random.randint(jax.random.fold_in(stream_key, axis), (), 0, length) for axis, length in enumerate(drawn.shape)]
        where[longest] = (where[longest] + shift) % drawn.shape[longest]
        spots.append(tuple(where))
    return drawn.at[spots[0]].set(smallest).at[spots[1]].set(largest)


def level_of(stream_key, extent, split, least, largest):
    def one(position, parts):
        steps = jax.random.uniform(jax.random.fold_in(jax.random.fold_in(stream_key, 6), position), (parts,), jnp.float32, least / len(split), largest / len(split))
        return jnp.repeat(jnp.exp(steps), extent[position] // parts).reshape((-1,) + (1,) * (len(extent) - position - 1))

    gain = one(*split[0])
    for cut in split[1:]:
        gain = gain * one(*cut)
    return gain


def shared_out(stream_key, own, number, rows, number_of, top, most, slope):
    sequence = jax.random.permutation(stream_key, number_of)
    heavy_load, usual = portions_of(number_of, rows * top, most, slope, True), portions_of(number_of, rows * top, most, slope, False)
    places = jnp.arange(number_of)

    def named(sizes, rotation):
        used = int((sizes > 0).sum())
        fixed = max(1, used // 4)
        moved = fixed + (places - fixed + rotation * (used - fixed)) % max(1, number_of - fixed)
        return jnp.zeros((number_of,), jnp.int32).at[sequence[jnp.where(places < fixed, places, moved)]].set(jnp.asarray(sizes, jnp.int32))

    sizes = jnp.where(number % 4 == 0, named(heavy_load, number // 4), named(usual, number - number // 4 - 1))
    mixed = jax.random.permutation(jax.random.fold_in(own, 3), number_of)
    donor, sink = mixed[0:number_of // 2 * 2:2], mixed[1:number_of // 2 * 2:2]
    room = jnp.minimum(sizes[donor] - 1, most - sizes[sink]) // 2
    room = jnp.where((donor == sequence[0]) | (sink == sequence[0]) | (sizes[sink] == 0), 0, jnp.maximum(room, 0))
    moved = jax.random.randint(jax.random.fold_in(own, 4), (number_of // 2,), 0, 1 << 20) % (room + 1)
    sizes = sizes.at[donor].add(-moved).at[sink].add(moved)
    items = jnp.searchsorted(jnp.cumsum(sizes), jnp.arange(rows * top), side="right").astype(jnp.int32)
    grid = items.reshape(top, rows).T
    grid = grid[jax.random.permutation(jax.random.fold_in(own, 1), rows)]
    rotation = jax.random.randint(jax.random.fold_in(own, 2), (rows, 1), 0, top)
    return jnp.take_along_axis(grid, (jnp.arange(top)[None, :] + rotation) % top, axis=1)


def portions_of(count, total, bound, lean, full):
    weights = [(1 << 20) // math.isqrt(grade ** lean) + 1 for grade in range(1, count + 1)]
    largest = bound if full else min(bound, max(-(-total // count), total * weights[0] // sum(weights)))
    least = 1 if total - largest >= count - 1 else 0
    given, spare = [largest] + [least] * (count - 1), total - largest - least * (count - 1)
    while spare > 0:
        free = [i for i in range(1, count) if given[i] < largest] or [i for i in range(1, count) if given[i] < bound]
        mass, remaining = sum([weights[i] for i in free]), spare
        for i in free:
            addition = min(bound - given[i], max(1, remaining * weights[i] // mass), spare)
            given[i] = given[i] + addition
            spare = spare - addition
    return np.array(given)


def scatter_about(rng, extent, width, limit, pieces=(), held_as=jnp.bfloat16):
    result = width * jax.random.normal(rng, extent, jnp.float32)
    if pieces:
        result = result * level_of(rng, extent, pieces, -0.22, 0.18)
    return jnp.clip(result, -limit, limit).astype(held_as)


def setup_inputs(seed: int = 0) -> dict:
    arg_keys = jax.random.split(jax.random.key(seed), 7)
    embeddings = scatter_about(arg_keys[0], (BATCH, EMBEDDING_WIDTH), 1.0, 6.0, ((0, 128),))
    labels = with_ends(jax.random.randint(arg_keys[1], (BATCH,), 0, SAMPLED), jax.random.fold_in(arg_keys[1], 1), 0, SAMPLED - 1).astype(jnp.int32)
    centres = scatter_about(arg_keys[2], (CLASSES, EMBEDDING_WIDTH), EMBEDDING_WIDTH ** -0.5, 0.25, ((0, 32),))
    momentum = scatter_about(arg_keys[3], (CLASSES, EMBEDDING_WIDTH), 0.5, 3.0, ((0, 32),), jnp.float32)
    sample_home_keys = jax.random.split(jax.random.fold_in(arg_keys[4], 1), SAMPLED // SAMP_DEV)
    sample_home_turns = jax.random.permutation(jax.random.fold_in(arg_keys[4], 3), SAMPLED // SAMP_DEV)
    sample_home = jax.vmap(lambda own, number: shared_out(jax.random.fold_in(arg_keys[4], 2), own, number, SAMP_DEV, N_CLS, 1, CAP, 2))(sample_home_keys, sample_home_turns).reshape((SAMPLED, 1))
    sample_row = with_ends(jax.random.randint(arg_keys[5], (SAMPLED,), 0, CLS_DEV), jax.random.fold_in(arg_keys[5], 1), 0, CLS_DEV - 1).astype(jnp.int32)
    return dict(embeddings=embeddings, labels=labels, centres=centres, momentum=momentum, sample_home=sample_home, sample_row=sample_row)


eps = 1e-06
logit_scale = 64.0
margin = 0.35
momentum_rate = 0.9
learn_rate = 0.1
weight_decay = 0.0005

def reference(embeddings, labels, centres, momentum, sample_home, sample_row):
    xfloat = embeddings.astype(jnp.float32)
    row_norm = jnp.sqrt(lax.optimization_barrier(jnp.sum(xfloat * xfloat, axis=1, keepdims=True)) + eps)
    unit_centres = xfloat / row_norm
    normalized_embedding = unit_centres.astype(jnp.bfloat16)
    columns = (sample_home[:, 0] * CLS_DEV + sample_row).astype(jnp.int32)
    fetched = centres[columns]
    wfloat = fetched.astype(jnp.float32)
    col_norm = jnp.sqrt(lax.optimization_barrier(jnp.sum(wfloat * wfloat, axis=1, keepdims=True)) + eps)
    wunit = wfloat / col_norm
    what = wunit.astype(jnp.bfloat16)
    rows_per_group = ROW_DEV * N_CLS
    grouped_embeddings = normalized_embedding.reshape(N_DP, rows_per_group, EMBEDDING_WIDTH)
    grouped_labels = labels.reshape(N_DP, rows_per_group)
    column_ids = jnp.arange(SAMPLED, dtype=jnp.int32)

    def one_group(carry, inputs):
        batch_rows, batch_labels = inputs
        cosine = lax.dot_general(batch_rows, what, (((1,), (1,)), ((), ())), preferred_element_type=jnp.float32)
        target = (batch_labels[:, None] == column_ids[None, :]).astype(jnp.float32)
        logit = logit_scale * (cosine - margin * target)
        exp_logit = jnp.exp(logit)
        denominator = lax.optimization_barrier(jnp.sum(exp_logit, axis=1, keepdims=True))
        grad_logit = (logit_scale * (exp_logit / denominator - target)).astype(jnp.bfloat16)
        dunit = jnp.dot(grad_logit, what, preferred_element_type=jnp.float32)
        partial_w = lax.dot_general(grad_logit, batch_rows, (((0,), (0,)), ((), ())), preferred_element_type=jnp.float32)
        return (carry + partial_w, dunit)
    dwhat, dunits = lax.scan(one_group, jnp.zeros((SAMPLED, EMBEDDING_WIDTH), jnp.float32), (grouped_embeddings, grouped_labels))
    dunit = dunits.reshape(N_DP * rows_per_group, EMBEDDING_WIDTH)
    emb_grad = (dunit - unit_centres * lax.optimization_barrier(jnp.sum(unit_centres * dunit, axis=1, keepdims=True))) / row_norm
    dfetched = (dwhat - wunit * lax.optimization_barrier(jnp.sum(wunit * dwhat, axis=1, keepdims=True))) / col_norm
    centre_grad = jnp.zeros((CLASSES, EMBEDDING_WIDTH), jnp.float32).at[columns].add(dfetched)
    momentum_new = momentum_rate * momentum + centre_grad + weight_decay * centres.astype(jnp.float32)
    centres_new = (centres.astype(jnp.float32) - learn_rate * momentum_new).astype(jnp.bfloat16)
    return (emb_grad, momentum_new, centres_new)
```

```python
import functools

import jax
import jax.numpy as jnp
from jax import lax
from jax.experimental import pallas as pl
from jax.experimental.pallas import tpu as pltpu
from jax.sharding import Mesh
from jax.sharding import PartitionSpec as P

CLS = ("cls_0", "cls_1", "cls_2")
DP_CLS = ("dp", "cls_0", "cls_1", "cls_2")

eps = 1e-06
logit_scale = 64.0
margin = 0.35
momentum_rate = 0.9
learn_rate = 0.1
weight_decay = 0.0005
BF16 = jnp.bfloat16
F32 = jnp.float32


def matmul(a, b):
    return jnp.dot(a, b, preferred_element_type=F32)


def plan_columns(home, row, groups, group, shards, slots):
    columns = home.shape[0]
    block = 128
    blocks = columns // block
    onehot = (home[:, None] == jnp.arange(shards)[None, :]).astype(BF16)
    cut = onehot.reshape(blocks, block, shards)
    lower = jnp.tril(jnp.ones((block, block), BF16), -1)
    within = jnp.einsum("ij,bjh->bih", lower, cut, preferred_element_type=F32)
    totals = jnp.sum(cut.astype(F32), axis=1)
    before = matmul(jnp.tril(jnp.ones((blocks, blocks), BF16), -1), totals.astype(BF16))
    count = jnp.sum(totals, axis=0)
    offset = jnp.sum(
        jnp.where(jnp.arange(shards)[:, None] < jnp.arange(shards)[None, :], count[:, None], 0.0), axis=0
    )
    table = (within + before[:, None, :] + offset[None, None, :]).reshape(columns, shards)
    onehot32 = onehot.astype(F32)
    place = jnp.sum(table * onehot32, axis=1).astype(jnp.int32)
    first = ((offset.astype(jnp.int32) - group + groups - 1) // groups).astype(F32)
    start = jnp.sum(first[None, :] * onehot32, axis=1).astype(jnp.int32)
    mine = place % groups == group
    kept = jnp.where(mine, place // groups, -1)
    slot = jnp.where(mine, home * slots + place // groups - start, -1)

    def digits(*values):
        parts = [part for value in values for part in (value // 64, value % 64)]
        return jnp.stack(parts, axis=1).astype(BF16)

    def whole(parts, i):
        return (parts[:, 2 * i] * 64 + parts[:, 2 * i + 1]).astype(jnp.int32)

    by_slot = (jnp.arange(shards * slots)[:, None] == slot[None, :]).astype(BF16)
    request = whole(matmul(by_slot, digits(row)), 0)
    by_kept = (jnp.arange(columns // groups)[:, None] == kept[None, :]).astype(BF16)
    found = matmul(by_kept, digits(slot, jnp.arange(columns)))
    return request, whole(found, 0), whole(found, 1)


def update_kernel(index_ref, returned_ref, momentum_ref, centres_ref, momentum_out, centres_out):
    rows = momentum_ref.shape[0]
    slots = returned_ref.shape[0]
    first = pl.program_id(0) * rows
    ids = lax.broadcasted_iota(jnp.int32, (rows, slots), 0) + first
    pick = jnp.where(ids == index_ref[...], 1.0, 0.0).astype(BF16)
    grad = jnp.dot(pick, returned_ref[...], preferred_element_type=F32)
    centre = centres_ref[...].astype(F32)
    momentum = momentum_rate * momentum_ref[...] + grad + weight_decay * centre
    momentum_out[...] = momentum
    centres_out[...] = (centre - learn_rate * momentum).astype(BF16)


def update(index, returned, momentum, centres, rows=512):
    slots, width = returned.shape
    homes = centres.shape[0]
    part = pl.BlockSpec((rows, width), lambda i: (i, 0))
    return pl.pallas_call(
        update_kernel,
        grid=(homes // rows,),
        in_specs=[
            pl.BlockSpec((1, slots), lambda i: (0, 0)),
            pl.BlockSpec((slots, width), lambda i: (0, 0)),
            part,
            part,
        ],
        out_specs=[part, part],
        out_shape=[
            jax.ShapeDtypeStruct((homes, width), F32),
            jax.ShapeDtypeStruct((homes, width), BF16),
        ],
        compiler_params=pltpu.CompilerParams(vmem_limit_bytes=48 * 2**20),
        cost_estimate=pl.CostEstimate(
            flops=2 * homes * slots * width, bytes_accessed=16 * homes * width, transcendentals=0
        ),
        name="update",
    )(index.reshape(1, slots), returned, momentum, centres)


def body(embeddings, labels, centres, momentum, sample_home, sample_row):
    shards = lax.axis_size(CLS)
    groups = lax.axis_size("dp")
    group = lax.axis_index("dp")
    tile = lax.axis_index(CLS)
    columns = sample_row.shape[0]
    slots = 2 * columns // shards // groups
    width = embeddings.shape[1]
    homes = centres.shape[0]

    xfloat = embeddings.astype(F32)
    row_norm = jnp.sqrt(jnp.sum(xfloat * xfloat, axis=1, keepdims=True) + eps)
    unit = xfloat / row_norm
    xhat = lax.all_gather(unit.astype(BF16), DP_CLS, axis=0, tiled=True)
    labels = lax.all_gather(labels, "dp", axis=0, tiled=True)

    request, slot, column = plan_columns(sample_home[:, 0], sample_row, groups, group, shards, slots)
    incoming = lax.all_to_all(request.reshape(shards, slots), CLS, split_axis=0, concat_axis=0, tiled=True)
    incoming = incoming.reshape(-1)
    pick = (incoming[:, None] == jnp.arange(homes)[None, :]).astype(BF16)
    replies = matmul(pick, centres).astype(BF16)
    arrived = lax.all_to_all(
        replies.reshape(shards, slots, width), CLS, split_axis=0, concat_axis=0, tiled=True
    ).reshape(shards * slots, width)
    index = lax.all_gather(incoming, "dp", axis=0, tiled=True)

    place = (slot[:, None] == jnp.arange(shards * slots)[None, :]).astype(BF16)
    wfloat = matmul(place, arrived)
    col_norm = jnp.sqrt(jnp.sum(wfloat * wfloat, axis=1, keepdims=True) + eps)
    wunit = wfloat / col_norm
    what = wunit.astype(BF16)
    cosine = lax.dot_general(xhat, what, (((1,), (1,)), ((), ())), preferred_element_type=F32)
    target = ((labels - tile * columns)[:, None] == column[None, :]).astype(F32)
    exp_logit = jnp.exp(logit_scale * (cosine - margin * target))
    denominator = lax.psum(jnp.sum(exp_logit, axis=1), DP_CLS)
    grad_logit = (logit_scale * (exp_logit / denominator[:, None] - target)).astype(BF16)
    dwhat = lax.dot_general(grad_logit, xhat, (((0,), (0,)), ((), ())), preferred_element_type=F32)
    dfetched = (dwhat - wunit * jnp.sum(wunit * dwhat, axis=1, keepdims=True)) / col_norm
    packed = lax.dot_general(
        place, dfetched.astype(BF16), (((0,), (0,)), ((), ())), preferred_element_type=F32
    ).astype(BF16)
    received = lax.all_to_all(
        packed.reshape(shards, slots, width), CLS, split_axis=0, concat_axis=0, tiled=True
    ).reshape(shards * slots, width)
    returned = lax.all_gather(received, "dp", axis=0, tiled=True)
    dunit = lax.psum_scatter(matmul(grad_logit, what), DP_CLS, scatter_dimension=0, tiled=True)
    emb_grad = (dunit - unit * jnp.sum(unit * dunit, axis=1, keepdims=True)) / row_norm
    momentum_new, centres_new = update(index, returned, momentum, centres)
    return (emb_grad, momentum_new, centres_new)


def solution(mesh):
    torus = Mesh(mesh.devices.reshape(mesh.shape["dp"], 4, 4, 2), ("dp", "cls_0", "cls_1", "cls_2"))
    return jax.shard_map(
        body,
        mesh=torus,
        in_specs=(P(DP_CLS, None), P("dp"), P(CLS, None), P(CLS, None), P(CLS, None), P(CLS)),
        out_specs=(P(DP_CLS, None), P(CLS, None), P(CLS, None)),
        check_vma=False,
    )
```

```python
import functools

import jax
import jax.numpy as jnp
from jax import lax
from jax.experimental import pallas as pl
from jax.experimental.pallas import tpu as pltpu
from jax.sharding import Mesh
from jax.sharding import PartitionSpec as P

CLS = ("cls_0", "cls_1", "cls_2")
DP_CLS = ("dp", "cls_0", "cls_1", "cls_2")

eps = 1e-06
logit_scale = 64.0
margin = 0.35
momentum_rate = 0.9
learn_rate = 0.1
weight_decay = 0.0005
BF16 = jnp.bfloat16
F32 = jnp.float32


def matmul(a, b):
    return jnp.dot(a, b, preferred_element_type=F32)


def plan_columns(home, row, groups, group, shards, slots):
    columns = home.shape[0]
    block = 128
    blocks = columns // block
    onehot = (home[:, None] == jnp.arange(shards)[None, :]).astype(BF16)
    cut = onehot.reshape(blocks, block, shards)
    lower = jnp.tril(jnp.ones((block, block), BF16), -1)
    within = jnp.einsum("ij,bjh->bih", lower, cut, preferred_element_type=F32)
    totals = jnp.sum(cut.astype(F32), axis=1)
    before = matmul(jnp.tril(jnp.ones((blocks, blocks), BF16), -1), totals.astype(BF16))
    count = jnp.sum(totals, axis=0)
    offset = jnp.sum(
        jnp.where(jnp.arange(shards)[:, None] < jnp.arange(shards)[None, :], count[:, None], 0.0), axis=0
    )
    table = (within + before[:, None, :] + offset[None, None, :]).reshape(columns, shards)
    onehot32 = onehot.astype(F32)
    place = jnp.sum(table * onehot32, axis=1).astype(jnp.int32)
    first = ((offset.astype(jnp.int32) - group + groups - 1) // groups).astype(F32)
    start = jnp.sum(first[None, :] * onehot32, axis=1).astype(jnp.int32)
    mine = place % groups == group
    kept = jnp.where(mine, place // groups, -1)
    slot = jnp.where(mine, home * slots + place // groups - start, -1)

    def digits(*values):
        parts = [part for value in values for part in (value // 64, value % 64)]
        return jnp.stack(parts, axis=1).astype(BF16)

    def whole(parts, i):
        return (parts[:, 2 * i] * 64 + parts[:, 2 * i + 1]).astype(jnp.int32)

    by_slot = (jnp.arange(shards * slots)[:, None] == slot[None, :]).astype(BF16)
    request = whole(matmul(by_slot, digits(row)), 0)
    by_kept = (jnp.arange(columns // groups)[:, None] == kept[None, :]).astype(BF16)
    found = matmul(by_kept, digits(slot, jnp.arange(columns)))
    return request, whole(found, 0), whole(found, 1)


def update_kernel(index_ref, returned_ref, momentum_ref, centres_ref, momentum_out, centres_out):
    rows = momentum_ref.shape[0]
    slots = returned_ref.shape[0]
    first = pl.program_id(0) * rows
    ids = lax.broadcasted_iota(jnp.int32, (rows, slots), 0) + first
    pick = jnp.where(ids == index_ref[...], 1.0, 0.0).astype(BF16)
    grad = jnp.dot(pick, returned_ref[...], preferred_element_type=F32)
    centre = centres_ref[...].astype(F32)
    momentum = momentum_rate * momentum_ref[...] + grad + weight_decay * centre
    momentum_out[...] = momentum
    centres_out[...] = (centre - learn_rate * momentum).astype(BF16)


def update(index, returned, momentum, centres, rows=512):
    slots, width = returned.shape
    homes = centres.shape[0]
    part = pl.BlockSpec((rows, width), lambda i: (i, 0))
    return pl.pallas_call(
        update_kernel,
        grid=(homes // rows,),
        in_specs=[
            pl.BlockSpec((1, slots), lambda i: (0, 0)),
            pl.BlockSpec((slots, width), lambda i: (0, 0)),
            part,
            part,
        ],
        out_specs=[part, part],
        out_shape=[
            jax.ShapeDtypeStruct((homes, width), F32),
            jax.ShapeDtypeStruct((homes, width), BF16),
        ],
        compiler_params=pltpu.CompilerParams(vmem_limit_bytes=48 * 2**20),
        cost_estimate=pl.CostEstimate(
            flops=2 * homes * slots * width, bytes_accessed=16 * homes * width, transcendentals=0
        ),
        name="update",
    )(index.reshape(1, slots), returned, momentum, centres)


MESH = pl.DeviceIdType.MESH
N_TILES = 32
ACROSS = 4


def where_am_i():
    z, y, x, c = (lax.axis_index(name) for name in DP_CLS)
    return z, y, x, c, y * 8 + x * 2 + c


def ahead(position, k):
    return lax.rem(position + k, ACROSS)


def tile_device(z, t):
    return (z, lax.div(t, 8), lax.rem(lax.div(t, 2), ACROSS), lax.rem(t, 2))


def remote(src, dst, send, recv, device):
    return pltpu.make_async_remote_copy(
        src_ref=src, dst_ref=dst, send_sem=send, recv_sem=recv, device_id=device, device_id_type=MESH
    )


def greet(devices, tiles=None):
    barrier = pltpu.get_barrier_semaphore()
    for device in devices:
        pl.semaphore_signal(barrier, inc=1, device_id=device, device_id_type=MESH)
    count = len(devices)
    if tiles is not None:
        z, me = tiles

        @pl.loop(1, N_TILES)
        def _(k):
            pl.semaphore_signal(
                barrier, inc=1, device_id=tile_device(z, lax.rem(me + k, N_TILES)), device_id_type=MESH
            )

        count += N_TILES - 1
    pl.semaphore_wait(barrier, count)


def fetch_kernel(
    request_ref, labels_ref, centres_ref, slot_ref, fetched_out, index_out, labels_out,
    incoming, index_all, labels_all, replies, arrived,
    request_sent, request_came, reply_sent, reply_came, index_sent, index_came, labels_sent, labels_came,
):
    z, y, x, c, me = where_am_i()
    homes = centres_ref.shape[0]
    slots = replies.shape[1]
    greet([(ahead(z, k), y, x, c) for k in range(1, ACROSS)], (z, me))

    def ask(k):
        t = lax.rem(me + k, N_TILES)
        return remote(
            request_ref.at[t], incoming.at[me], request_sent.at[t], request_came.at[me], tile_device(z, t)
        )

    def answer(t):
        return remote(replies.at[t], arrived.at[me], reply_sent.at[t], reply_came.at[me], tile_device(z, t))

    def answered(t):
        return remote(replies.at[t], arrived.at[t], reply_sent.at[t], reply_came.at[t], tile_device(z, t))

    def asked(t):
        return remote(request_ref.at[t], incoming.at[t], request_sent.at[t], request_came.at[t], tile_device(z, t))

    @pl.loop(1, N_TILES)
    def _(k):
        ask(k).start()

    tell = [
        remote(labels_ref, labels_all.at[k], labels_sent.at[k], labels_came.at[k], (ahead(z, k + 1), y, x, c))
        for k in range(ACROSS - 1)
    ]
    for copy in tell:
        copy.start()
    incoming[me] = request_ref[me]

    @pl.loop(1, N_TILES)
    def _(k):
        asked(lax.rem(me + k, N_TILES)).wait_recv()

    share = [
        remote(incoming, index_all.at[k], index_sent.at[k], index_came.at[k], (ahead(z, k + 1), y, x, c))
        for k in range(ACROSS - 1)
    ]
    for copy in share:
        copy.start()
    row_ids = lax.broadcasted_iota(jnp.int32, (slots, homes), 1)
    for q in (1, 2, 3, 0):
        first = ahead(y, q) * 8
        wanted = incoming[pl.ds(first, 8)].reshape(8, 128).T
        pick = jnp.concatenate(
            [jnp.where(row_ids == wanted[:slots, j : j + 1], 1.0, 0.0).astype(BF16) for j in range(8)], axis=0
        )
        found = jnp.dot(pick, centres_ref[...], preferred_element_type=F32).astype(BF16)
        replies[pl.ds(first, 8)] = found.reshape(8, slots, found.shape[1])
        for j in range(8):
            if q:
                answer(first + j).start()
            else:

                @pl.when(first + j != me)
                def _(t=first + j):
                    answer(t).start()

    arrived[me] = replies[me]
    index_out[z] = incoming[...]
    labels_out[z] = labels_ref[...]
    for k in range(ACROSS - 1):
        source = ahead(z, ACROSS - 1 - k)
        tell[k].wait()
        labels_out[source] = labels_all[k]
        share[k].wait()
        index_out[source] = index_all[k]

    @pl.loop(1, N_TILES)
    def _(k):
        answered(lax.rem(me + k, N_TILES)).wait_recv()

    kept = slot_ref.shape[0]
    place = slot_ref[...] == lax.broadcasted_iota(jnp.int32, (kept, N_TILES * slots), 1)
    place = jnp.where(place, 1.0, 0.0).astype(BF16)
    rows = arrived[...].reshape(N_TILES * slots, arrived.shape[2])
    fetched_out[...] = jnp.dot(place, rows, preferred_element_type=F32).astype(BF16)

    @pl.loop(1, N_TILES)
    def _(k):
        ask(k).wait_send()
        answer(lax.rem(me + k, N_TILES)).wait_send()


def fetch(request, labels, centres, slot, slots):
    kept, width = slot.shape[0], centres.shape[1]
    vmem = pl.BlockSpec(memory_space=pltpu.VMEM)
    return pl.pallas_call(
        fetch_kernel,
        in_specs=[vmem] * 4,
        out_specs=[vmem] * 3,
        out_shape=[
            jax.ShapeDtypeStruct((kept, width), BF16),
            jax.ShapeDtypeStruct((ACROSS, N_TILES, 1, 128), jnp.int32),
            jax.ShapeDtypeStruct((ACROSS, 16, 128), jnp.int32),
        ],
        scratch_shapes=[
            pltpu.VMEM((N_TILES, 1, 128), jnp.int32),
            pltpu.VMEM((ACROSS - 1, N_TILES, 1, 128), jnp.int32),
            pltpu.VMEM((ACROSS - 1, 16, 128), jnp.int32),
            pltpu.VMEM((N_TILES, slots, width), BF16),
            pltpu.VMEM((N_TILES, slots, width), BF16),
        ]
        + [pltpu.SemaphoreType.DMA((N_TILES,))] * 4
        + [pltpu.SemaphoreType.DMA((ACROSS - 1,))] * 4,
        compiler_params=pltpu.CompilerParams(
            collective_id=0, has_side_effects=True, vmem_limit_bytes=40 * 2**20
        ),
        name="fetch",
    )(request, labels, centres, slot)


def margin_kernel(
    xhalf_ref, fetched_ref, labels_ref, column_ref, slot_ref, received_out, grad_out, turned_out,
    xall, expo, den, got, inverse, acc, wunit, packed, arrived,
    x_here, x_sent, x_came, den_sent, den_came, row_sent, row_came,
):
    z, y, x, c, me = where_am_i()
    other = 1 - c
    partner = (z, y, x, other)
    along = {
        "x": [(z, y, ahead(x, k), c) for k in range(1, ACROSS)],
        "y": [(z, ahead(y, k), x, c) for k in range(1, ACROSS)],
        "z": [(ahead(z, k), y, x, c) for k in range(1, ACROSS)],
    }
    greet(along["z"], (z, me))
    pieces = 8
    slots = packed.shape[1]

    def piece_here(i):
        two = pl.ds(2 * i, 2)
        return pltpu.make_async_copy(xhalf_ref.at[:, two], xall.at[c, :, two], x_here.at[i])

    def piece_over(i, slot):
        two = pl.ds(2 * i, 2)
        return remote(xhalf_ref.at[:, two], xall.at[slot, :, two], x_sent.at[i], x_came.at[i], partner)

    @pl.loop(0, pieces)
    def _(i):
        piece_here(i).start()
        piece_over(i, c).start()

    wfloat = fetched_ref[...].astype(F32)
    col_norm = jnp.sqrt(jnp.sum(wfloat * wfloat, axis=1, keepdims=True) + eps)
    wunit[...] = wfloat / col_norm
    turned_out[...] = wunit[...].T.astype(BF16)

    def rows_of(side, i):
        return jnp.concatenate([xall[side, g, 2 * i + j] for j in range(2) for g in range(ACROSS)], axis=0)

    def exponents(side, i):
        b = side * pieces + i
        cosine = lax.dot_general(
            wunit[...].astype(BF16), rows_of(side, i), (((1,), (1,)), ((), ())), preferred_element_type=F32
        )
        hit = column_ref[...] == labels_ref[pl.ds(b, 1)]
        value = jnp.exp(logit_scale * jnp.where(hit, cosine - margin, cosine))
        expo[b] = value
        den[0, pl.ds(b, 1)] = jnp.sum(value, axis=0, keepdims=True)

    @pl.loop(0, pieces)
    def _(i):
        piece_here(i).wait()
        exponents(c, i)

    @pl.loop(0, pieces)
    def _(i):
        piece_over(i, other).wait_recv()
        exponents(other, i)

    slot = 0
    for stage, peers in enumerate(([partner], along["x"], along["y"], along["z"])):
        copies = [
            remote(den.at[stage], got.at[slot + k], den_sent.at[slot + k], den_came.at[slot + k], peer)
            for k, peer in enumerate(peers)
        ]
        for copy in copies:
            copy.start()
        for copy in copies:
            copy.wait()
        total = den[stage]
        for k in range(len(peers)):
            total = total + got[slot + k]
        if stage < 3:
            den[stage + 1] = total
        else:
            inverse[...] = logit_scale / total
        slot += len(peers)

    acc[...] = jnp.zeros_like(acc)

    @pl.loop(0, 2 * pieces)
    def _(b):
        hit = column_ref[...] == labels_ref[pl.ds(b, 1)]
        share = expo[b] * inverse[pl.ds(b, 1)]
        grad = jnp.where(hit, share - logit_scale, share).astype(BF16)
        grad_out[b] = grad
        acc[...] += jnp.dot(grad, rows_of(lax.div(b, pieces), lax.rem(b, pieces)), preferred_element_type=F32)

    dwhat = acc[...]
    unit = wunit[...]
    wfloat = fetched_ref[...].astype(F32)
    col_norm = jnp.sqrt(jnp.sum(wfloat * wfloat, axis=1, keepdims=True) + eps)
    dfetched = ((dwhat - unit * jnp.sum(unit * dwhat, axis=1, keepdims=True)) / col_norm).astype(BF16)
    kept = dfetched.shape[0]
    place = slot_ref[...] == lax.broadcasted_iota(jnp.int32, (N_TILES * slots, kept), 0)
    place = jnp.where(place, 1.0, 0.0).astype(BF16)
    rows = jnp.dot(place, dfetched, preferred_element_type=F32).astype(BF16)
    packed[...] = rows.reshape(packed.shape)

    def give(t):
        return remote(packed.at[t], arrived.at[me], row_sent.at[t], row_came.at[me], tile_device(z, t))

    def given(t):
        return remote(packed.at[t], arrived.at[t], row_sent.at[t], row_came.at[t], tile_device(z, t))

    @pl.loop(1, N_TILES)
    def _(k):
        give(lax.rem(me + k, N_TILES)).start()

    arrived[me] = packed[me]

    @pl.loop(0, pieces)
    def _(i):
        piece_over(i, c).wait_send()

    @pl.loop(1, N_TILES)
    def _(k):
        given(lax.rem(me + k, N_TILES)).wait_recv()

    received_out[...] = arrived[...]

    @pl.loop(1, N_TILES)
    def _(k):
        give(lax.rem(me + k, N_TILES)).wait_send()


def margin_step(xhalf, fetched, labels, column, slot, slots):
    kept, width = fetched.shape
    blocks, block = labels.shape
    vmem = pl.BlockSpec(memory_space=pltpu.VMEM)
    return pl.pallas_call(
        margin_kernel,
        in_specs=[pl.BlockSpec(memory_space=pl.ANY)] + [vmem] * 4,
        out_specs=[vmem] * 3,
        out_shape=[
            jax.ShapeDtypeStruct((N_TILES, slots, width), BF16),
            jax.ShapeDtypeStruct((blocks, kept, block), BF16),
            jax.ShapeDtypeStruct((width, kept), BF16),
        ],
        scratch_shapes=[
            pltpu.VMEM((2, *xhalf.shape), BF16),
            pltpu.VMEM((blocks, kept, block), F32),
            pltpu.VMEM((4, blocks, block), F32),
            pltpu.VMEM((10, blocks, block), F32),
            pltpu.VMEM((blocks, block), F32),
            pltpu.VMEM((kept, width), F32),
            pltpu.VMEM((kept, width), F32),
            pltpu.VMEM((N_TILES, slots, width), BF16),
            pltpu.VMEM((N_TILES, slots, width), BF16),
        ]
        + [pltpu.SemaphoreType.DMA((8,))] * 3
        + [pltpu.SemaphoreType.DMA((10,))] * 2
        + [pltpu.SemaphoreType.DMA((N_TILES,))] * 2,
        compiler_params=pltpu.CompilerParams(
            collective_id=1, has_side_effects=True, vmem_limit_bytes=56 * 2**20
        ),
        name="margin_step",
    )(xhalf, fetched, labels, column, slot)


def reduce_kernel(
    grad_ref, turned_ref, dunit_out, over, came, mine, first_a, first_b, next_a, next_b, second_a, second_b, last, third,
    over_sent, over_came, step_sent, step_came,
):
    z, y, x, c, _ = where_am_i()
    other = 1 - c
    along_x = [(z, y, ahead(x, k), c) for k in range(1, ACROSS)]
    along_y = [(z, ahead(y, k), x, c) for k in range(1, ACROSS)]
    along_z = [(ahead(z, k), y, x, c) for k in range(1, ACROSS)]
    partner = (z, y, x, other)
    greet([partner] + along_x + along_y + along_z)
    pieces = 8
    half = mine.shape[2] // 2
    low, high = pl.ds(0, half), pl.ds(half, half)
    others = range(ACROSS - 1)

    def product(side, i):
        return jnp.dot(turned_ref[...], grad_ref[side * pieces + i], preferred_element_type=F32)

    def hand_over(i):
        two = pl.ds(2 * i, 2)
        return remote(over.at[two], came.at[two], over_sent.at[i], over_came.at[i], partner)

    @pl.loop(0, pieces)
    def _(i):
        part = product(other, i).astype(BF16)
        over[2 * i] = part[:, : part.shape[1] // 2]
        over[2 * i + 1] = part[:, part.shape[1] // 2 :]
        hand_over(i).start()

    @pl.loop(0, pieces)
    def _(i):
        part = product(c, i)
        hand_over(i).wait_recv()
        lanes = part.shape[1] // 2
        row, column = lax.div(i, 2), 2 * lax.rem(i, 2)
        mine[row, column] = (part[:, :lanes] + came[2 * i].astype(F32)).astype(BF16)
        mine[row, column + 1] = (part[:, lanes:] + came[2 * i + 1].astype(F32)).astype(BF16)

    def step(n, src, dst, device):
        return remote(src, dst, step_sent.at[n], step_came.at[n], device)

    one_a = [step(k, mine.at[:, ahead(x, k + 1), low], first_a.at[k], along_x[k]) for k in others]
    one_b = [step(3 + k, mine.at[ahead(y, k + 1), :, high], first_b.at[k], along_y[k]) for k in others]
    for copy in one_a + one_b:
        copy.start()
    for copy in one_a:
        copy.wait_recv()

    @pl.loop(0, ACROSS)
    def _(i):
        total = mine[i, x, low].astype(F32)
        for k in others:
            total = total + first_a[k, i].astype(F32)
        next_a[i] = total.astype(BF16)

    for copy in one_b:
        copy.wait_recv()

    @pl.loop(0, ACROSS)
    def _(i):
        total = mine[y, i, high].astype(F32)
        for k in others:
            total = total + first_b[k, i].astype(F32)
        next_b[i] = total.astype(BF16)

    two_a = [step(6 + k, next_a.at[ahead(y, k + 1)], second_a.at[k], along_y[k]) for k in others]
    two_b = [step(9 + k, next_b.at[ahead(x, k + 1)], second_b.at[k], along_x[k]) for k in others]
    for copy in two_a + two_b:
        copy.start()
    for copy in two_a + two_b:
        copy.wait_recv()
    top, bottom = next_a[y].astype(F32), next_b[x].astype(F32)
    for k in others:
        top = top + second_a[k].astype(F32)
        bottom = bottom + second_b[k].astype(F32)
    rows = last.shape[1]
    last[:, :, :half] = top.T.astype(BF16).reshape(ACROSS, rows, half)
    last[:, :, half:] = bottom.T.astype(BF16).reshape(ACROSS, rows, half)
    three = [step(12 + k, last.at[ahead(z, k + 1)], third.at[k], along_z[k]) for k in others]
    for copy in three:
        copy.start()
    for copy in three:
        copy.wait_recv()
    total = last[z].astype(F32)
    for k in others:
        total = total + third[k].astype(F32)
    dunit_out[...] = total
    for copy in one_a + one_b + two_a + two_b + three:
        copy.wait_send()

    @pl.loop(0, pieces)
    def _(i):
        hand_over(i).wait_send()


def reduce_dunit(grad, turned, rows):
    blocks, kept, block = grad.shape
    width = turned.shape[0]
    half, lanes = width // 2, block // 2
    vmem = pl.BlockSpec(memory_space=pltpu.VMEM)
    return pl.pallas_call(
        reduce_kernel,
        in_specs=[vmem] * 2,
        out_specs=vmem,
        out_shape=jax.ShapeDtypeStruct((rows, width), F32),
        scratch_shapes=[
            pltpu.VMEM((blocks, width, lanes), BF16),
            pltpu.VMEM((blocks, width, lanes), BF16),
            pltpu.VMEM((ACROSS, ACROSS, width, lanes), BF16),
            pltpu.VMEM((3, ACROSS, half, lanes), BF16),
            pltpu.VMEM((3, ACROSS, half, lanes), BF16),
            pltpu.VMEM((ACROSS, half, lanes), BF16),
            pltpu.VMEM((ACROSS, half, lanes), BF16),
            pltpu.VMEM((3, half, lanes), BF16),
            pltpu.VMEM((3, half, lanes), BF16),
            pltpu.VMEM((ACROSS, rows, width), BF16),
            pltpu.VMEM((3, rows, width), BF16),
            pltpu.SemaphoreType.DMA((8,)),
            pltpu.SemaphoreType.DMA((8,)),
            pltpu.SemaphoreType.DMA((15,)),
            pltpu.SemaphoreType.DMA((15,)),
        ],
        compiler_params=pltpu.CompilerParams(
            collective_id=2, has_side_effects=True, vmem_limit_bytes=48 * 2**20
        ),
        cost_estimate=pl.CostEstimate(
            flops=2 * blocks * block * kept * width, bytes_accessed=2**26, transcendentals=0
        ),
        name="reduce_dunit",
    )(grad, turned)


def body(embeddings, labels, centres, momentum, sample_home, sample_row):
    shards = lax.axis_size(CLS)
    groups = lax.axis_size("dp")
    group = lax.axis_index("dp")
    tile = lax.axis_index(CLS)
    columns = sample_row.shape[0]
    slots = 2 * columns // shards // groups
    rows, width = embeddings.shape

    xfloat = embeddings.astype(F32)
    row_norm = jnp.sqrt(jnp.sum(xfloat * xfloat, axis=1, keepdims=True) + eps)
    unit = xfloat / row_norm
    xhalf = lax.all_gather(unit.astype(BF16), ("dp", "cls_0", "cls_1"), axis=0, tiled=True)

    request, slot, column = plan_columns(sample_home[:, 0], sample_row, groups, group, shards, slots)
    request = jnp.pad(request.reshape(shards, 1, slots), ((0, 0), (0, 0), (0, 128 - slots)))
    fetched, index, labels = fetch(request, labels.reshape(16, 128), centres, slot[:, None], slots)
    labels = labels.reshape(groups, 16, 2, rows).transpose(2, 1, 0, 3).reshape(16, -1) - tile * columns
    received, grad, turned = margin_step(
        xhalf.reshape(groups, 16, rows, width), fetched, labels, column[:, None], slot[None, :], slots
    )
    returned = lax.all_gather(received.reshape(shards * slots, width), "dp", axis=0, tiled=True)
    dunit = reduce_dunit(grad, turned, rows)
    emb_grad = (dunit - unit * jnp.sum(unit * dunit, axis=1, keepdims=True)) / row_norm
    momentum_new, centres_new = update(index[:, :, 0, :slots].reshape(-1), returned, momentum, centres)
    return (emb_grad, momentum_new, centres_new)


def solution(mesh):
    torus = Mesh(mesh.devices.reshape(mesh.shape["dp"], 4, 4, 2), ("dp", "cls_0", "cls_1", "cls_2"))
    return jax.shard_map(
        body,
        mesh=torus,
        in_specs=(P(DP_CLS, None), P("dp"), P(CLS, None), P(CLS, None), P(CLS, None), P(CLS)),
        out_specs=(P(DP_CLS, None), P(CLS, None), P(CLS, None)),
        check_vma=False,
    )
```

```python
import jax
import jax.numpy as jnp
from jax import lax
from jax.experimental import pallas as pl
from jax.experimental.pallas import tpu as pltpu
from jax.sharding import Mesh
from jax.sharding import PartitionSpec as P

CLS = ("cls_0", "cls_1", "cls_2")
DP_CLS = ("dp", "cls_0", "cls_1", "cls_2")

eps = 1e-06
logit_scale = 64.0
margin = 0.35
momentum_rate = 0.9
learn_rate = 0.1
weight_decay = 0.0005
BF16 = jnp.bfloat16
F32 = jnp.float32


MESH = pl.DeviceIdType.MESH
N_TILES = 32
ACROSS = 4


def where_am_i():
    z, y, x, c = (lax.axis_index(name) for name in DP_CLS)
    return z, y, x, c, y * 8 + x * 2 + c


def ahead(position, k):
    return lax.rem(position + k, ACROSS)


def tile_device(z, t):
    return (z, lax.div(t, 8), lax.rem(lax.div(t, 2), ACROSS), lax.rem(t, 2))


def remote(src, dst, send, recv, device):
    return pltpu.make_async_remote_copy(
        src_ref=src, dst_ref=dst, send_sem=send, recv_sem=recv, device_id=device, device_id_type=MESH
    )


def greet(devices, tiles=None):
    barrier = pltpu.get_barrier_semaphore()
    for device in devices:
        pl.semaphore_signal(barrier, inc=1, device_id=device, device_id_type=MESH)
    count = len(devices)
    if tiles is not None:
        z, me = tiles

        @pl.loop(1, N_TILES)
        def _(k):
            pl.semaphore_signal(
                barrier, inc=1, device_id=tile_device(z, lax.rem(me + k, N_TILES)), device_id_type=MESH
            )

        count += N_TILES - 1
    pl.semaphore_wait(barrier, count)


def by_lanes(a, b):
    return lax.dot_general(a, b, (((1,), (1,)), ((), ())), preferred_element_type=F32)


def flag(condition):
    return jnp.where(condition, 1.0, 0.0)


def iota(shape, dim):
    return lax.broadcasted_iota(jnp.int32, shape, dim)


def plan_columns(home, row, group, slots):
    columns = home.shape[1]
    block = 128
    cuts = [slice(b * block, (b + 1) * block) for b in range(columns // block)]
    at_home = flag(iota((N_TILES, columns), 0) == home)
    upper = flag(iota((block, block), 0) < iota((block, block), 1)).astype(BF16)
    stacked = jnp.concatenate([at_home[:, cut] for cut in cuts], axis=0).astype(BF16)
    within = jnp.dot(stacked, upper, preferred_element_type=F32)
    before = [jnp.zeros((N_TILES, 1), F32)]
    for cut in cuts:
        before.append(before[-1] + jnp.sum(at_home[:, cut], axis=1, keepdims=True))
    count = jnp.broadcast_to(before[-1], (N_TILES, block)).astype(BF16)
    lower = flag(iota((N_TILES, N_TILES), 1) < iota((N_TILES, N_TILES), 0)).astype(BF16)
    offset = jnp.dot(lower, count, preferred_element_type=F32)
    first = ((offset.astype(jnp.int32) + (ACROSS - 1 - group)) >> 2).astype(F32)
    places, starts = [], []
    for b, cut in enumerate(cuts):
        mark = at_home[:, cut]
        rank = within[b * N_TILES : (b + 1) * N_TILES] + before[b] + offset
        places.append(jnp.sum(mark * rank, axis=0, keepdims=True))
        starts.append(jnp.sum(mark * first, axis=0, keepdims=True))
    place = jnp.concatenate(places, axis=1).astype(jnp.int32)
    start = jnp.concatenate(starts, axis=1).astype(jnp.int32)
    mine = (place & 3) == group
    kept = place >> 2
    slot = kept - start
    by_slot = flag(mine & (iota((block, columns), 0) == slot)).astype(BF16)
    digits = [at_home * (row >> 6).astype(F32), at_home * (row & 63).astype(F32)]
    asked = by_lanes(jnp.concatenate(digits, axis=0).astype(BF16), by_slot)
    request = (asked[:N_TILES] * 64 + asked[N_TILES:]).astype(jnp.int32)
    by_kept = flag(mine & (iota((block, columns), 0) == (kept & 127))).astype(BF16)
    lane = iota((1, columns), 1)
    parts = []
    for value in (home, slot, lane >> 6, lane & 63):
        for a in range(ACROSS):
            parts.append(jnp.where((kept >> 7) == a, value.astype(F32), 0.0))
    found = by_lanes(jnp.concatenate(parts, axis=0).astype(BF16), by_kept)
    turned = jnp.concatenate([found, jnp.zeros((block - found.shape[0], block), F32)], axis=0).T
    runs = range(ACROSS)
    slot_row = jnp.concatenate([found[a : a + 1] * slots + found[4 + a : 5 + a] for a in runs], axis=1)
    slot_column = jnp.concatenate([turned[:, a : a + 1] * slots + turned[:, 4 + a : 5 + a] for a in runs], axis=0)
    column = jnp.concatenate([turned[:, 8 + a : 9 + a] * 64 + turned[:, 12 + a : 13 + a] for a in runs], axis=0)
    return request, slot_row.astype(jnp.int32), slot_column.astype(jnp.int32), column.astype(jnp.int32)


def fetch_kernel(
    emb_ref, home_ref, row_ref, labels_ref, centres_hbm,
    xhalf, fetched_out, column_out, slot_out, index_out, labels_out,
    xhat, centres, request, incoming, index_all, labels_all, replies, arrived,
    local_sem, request_sent, request_came, reply_sent, reply_came, index_sent, index_came, labels_sent, labels_came,
    phase_sent, phase_came,
):
    z, y, x, c, me = where_am_i()
    homes = centres.shape[0]
    slots = replies.shape[1]
    load = pltpu.make_async_copy(centres_hbm, centres, local_sem.at[0])
    load.start()
    xfloat = emb_ref[...].astype(F32)
    row_norm = jnp.sqrt(jnp.sum(xfloat * xfloat, axis=1, keepdims=True) + eps)
    xhat[...] = (xfloat / row_norm).astype(BF16)
    keep = pltpu.make_async_copy(xhat, xhalf.at[z, y, x], local_sem.at[1])
    keep.start()
    asked, slot_row, slot_column, column = plan_columns(home_ref[...], row_ref[...], z, slots)
    request[...] = asked.reshape(request.shape)
    slot_out[...] = slot_row
    column_out[...] = column
    greet([(ahead(z, k), y, x, c) for k in range(1, ACROSS)], (z, me))

    def along(axis, k):
        return {"x": (z, y, ahead(x, k), c), "y": (z, ahead(y, k), x, c), "z": (ahead(z, k), y, x, c)}[axis]

    def ask(k):
        t = lax.rem(me + k, N_TILES)
        return remote(request.at[t], incoming.at[me], request_sent.at[t], request_came.at[me], tile_device(z, t))

    def asked_by(t):
        return remote(request.at[t], incoming.at[t], request_sent.at[t], request_came.at[t], tile_device(z, t))

    def answer(t):
        return remote(replies.at[t], arrived.at[me], reply_sent.at[t], reply_came.at[me], tile_device(z, t))

    def answered(t):
        return remote(replies.at[t], arrived.at[t], reply_sent.at[t], reply_came.at[t], tile_device(z, t))

    @pl.loop(1, N_TILES)
    def _(k):
        ask(k).start()

    def spread(part, phase):
        first, size, axes = ((0, 16, "zxy"), (16, 16, "zyx"), (32, 32, "xyz"))[part]
        done = axes[:phase]
        if phase == 0:
            src = xhat.at[pl.ds(first, size)]
            dst = xhalf.at[z, y, x, pl.ds(first, size)]
        else:
            everything = pl.ds(0, ACROSS)
            where = [everything if a in done else p for a, p in zip("zyx", (z, y, x))]
            src = dst = xhalf.at[where[0], where[1], where[2], pl.ds(first, size)]
        copies = []
        for k in range(ACROSS - 1):
            n = (part * 3 + phase) * 3 + k
            copies.append(remote(src, dst, phase_sent.at[n], phase_came.at[n], along(axes[phase], k + 1)))
        return copies

    waves = [[spread(part, phase) for part in range(3)] for phase in range(3)]
    flying = []

    def send(copies):
        for copy in copies:
            copy.start()
        flying.extend(copies)

    def land(copies):
        for copy in copies:
            copy.wait_recv()

    tell = [
        remote(labels_ref, labels_all.at[k], labels_sent.at[k], labels_came.at[k], along("z", k + 1))
        for k in range(ACROSS - 1)
    ]
    send(waves[0][2])
    send(waves[0][0])
    send(waves[0][1])
    send(tell)
    incoming[me] = request[me]

    @pl.loop(1, N_TILES)
    def _(k):
        asked_by(lax.rem(me + k, N_TILES)).wait_recv()

    share = [
        remote(incoming, index_all.at[k], index_sent.at[k], index_came.at[k], along("z", k + 1))
        for k in range(ACROSS - 1)
    ]
    send(share)
    keep.wait()
    for part in (2, 0, 1):
        land(waves[0][part])
        send(waves[1][part])
    load.wait()
    row_ids = iota((slots, homes), 1)
    for q in (1, 2, 3, 0):
        first = ahead(y, q) * 8
        wanted = incoming[pl.ds(first, 8)].reshape(8, 128).T
        pick = jnp.concatenate(
            [flag(row_ids == wanted[:slots, j : j + 1]).astype(BF16) for j in range(8)], axis=0
        )
        found = jnp.dot(pick, centres[...], preferred_element_type=F32).astype(BF16)
        replies[pl.ds(first, 8)] = found.reshape(8, slots, found.shape[1])
        for j in range(8):
            if q:
                answer(first + j).start()
            else:

                @pl.when(first + j != me)
                def _(t=first + j):
                    answer(t).start()

        part = {1: 2, 2: 0, 3: 1}.get(q)
        if part is not None:
            land(waves[1][part])
            send(waves[2][part])

    arrived[me] = replies[me]
    index_out[z] = incoming[...]
    labels_out[z] = labels_ref[...]
    land(tell + share)
    for k in range(ACROSS - 1):
        source = ahead(z, ACROSS - 1 - k)
        labels_out[source] = labels_all[k]
        index_out[source] = index_all[k]

    @pl.loop(1, N_TILES)
    def _(k):
        answered(lax.rem(me + k, N_TILES)).wait_recv()

    kept = slot_column.shape[0]
    place = flag(slot_column == iota((kept, N_TILES * slots), 1)).astype(BF16)
    rows = arrived[...].reshape(N_TILES * slots, arrived.shape[2])
    fetched_out[...] = jnp.dot(place, rows, preferred_element_type=F32).astype(BF16)
    for part in (0, 1, 2):
        land(waves[2][part])
    for copy in flying:
        copy.wait_send()

    @pl.loop(1, N_TILES)
    def _(k):
        ask(k).wait_send()
        answer(lax.rem(me + k, N_TILES)).wait_send()


def fetch(embeddings, home, row, labels, centres, kept, slots):
    rows, width = embeddings.shape
    vmem, anywhere = pl.BlockSpec(memory_space=pltpu.VMEM), pl.BlockSpec(memory_space=pl.ANY)
    return pl.pallas_call(
        fetch_kernel,
        in_specs=[vmem] * 4 + [anywhere],
        out_specs=[anywhere] + [vmem] * 5,
        out_shape=[
            jax.ShapeDtypeStruct((ACROSS, ACROSS, ACROSS, rows, width), BF16),
            jax.ShapeDtypeStruct((kept, width), BF16),
            jax.ShapeDtypeStruct((kept, 1), jnp.int32),
            jax.ShapeDtypeStruct((1, kept), jnp.int32),
            jax.ShapeDtypeStruct((ACROSS, N_TILES, 1, 128), jnp.int32),
            jax.ShapeDtypeStruct((ACROSS, 16, 128), jnp.int32),
        ],
        scratch_shapes=[
            pltpu.VMEM((rows, width), BF16),
            pltpu.VMEM(centres.shape, BF16),
            pltpu.VMEM((N_TILES, 1, 128), jnp.int32),
            pltpu.VMEM((N_TILES, 1, 128), jnp.int32),
            pltpu.VMEM((ACROSS - 1, N_TILES, 1, 128), jnp.int32),
            pltpu.VMEM((ACROSS - 1, 16, 128), jnp.int32),
            pltpu.VMEM((N_TILES, slots, width), BF16),
            pltpu.VMEM((N_TILES, slots, width), BF16),
            pltpu.SemaphoreType.DMA((2,)),
        ]
        + [pltpu.SemaphoreType.DMA((N_TILES,))] * 4
        + [pltpu.SemaphoreType.DMA((ACROSS - 1,))] * 4
        + [pltpu.SemaphoreType.DMA((27,))] * 2,
        compiler_params=pltpu.CompilerParams(
            collective_id=0, has_side_effects=True, vmem_limit_bytes=40 * 2**20
        ),
        name="fetch",
    )(embeddings, home, row, labels, centres)


def margin_kernel(
    xhalf_ref, fetched_ref, labels_ref, column_ref, slot_ref, index_ref, emb_ref, grads_hbm, emb_out,
    xall, expo, den, got, inverse, acc, wunit, turned, packed, arrived, nearby,
    over, came, mine, first_a, first_b, next_a, next_b, second_a, second_b, last, third,
    x_here, x_sent, x_came, den_sent, den_came, row_sent, row_came, ring_sent, ring_came,
    over_sent, over_came, step_sent, step_came, out_sem,
):
    z, y, x, c, me = where_am_i()
    other = 1 - c
    partner = (z, y, x, other)
    others = range(ACROSS - 1)
    along_x = [(z, y, ahead(x, k + 1), c) for k in others]
    along_y = [(z, ahead(y, k + 1), x, c) for k in others]
    along_z = [(ahead(z, k + 1), y, x, c) for k in others]
    greet(along_z, (z, me))
    pieces = 8
    slots = packed.shape[1]

    def piece_here(i):
        two = pl.ds(2 * i, 2)
        return pltpu.make_async_copy(xhalf_ref.at[:, two], xall.at[c, :, two], x_here.at[i])

    def piece_over(i, slot):
        two = pl.ds(2 * i, 2)
        return remote(xhalf_ref.at[:, two], xall.at[slot, :, two], x_sent.at[i], x_came.at[i], partner)

    @pl.loop(0, pieces)
    def _(i):
        piece_over(i, c).start()
        piece_here(i).start()

    def column_norm():
        wfloat = fetched_ref[...].astype(F32)
        return wfloat, jnp.sqrt(jnp.sum(wfloat * wfloat, axis=1, keepdims=True) + eps)

    wfloat, col_norm = column_norm()
    wunit[...] = wfloat / col_norm
    turned[...] = wunit[...].T.astype(BF16)

    def rows_of(side, i):
        return jnp.concatenate([xall[side, g, 2 * i + j] for j in range(2) for g in range(ACROSS)], axis=0)

    def exponents(group, i):
        @pl.when(c == 0)
        def _():
            piece_here(i).wait()

        @pl.when(c == 1)
        def _():
            piece_over(i, other).wait_recv()

        for side in range(2):
            if side:

                @pl.when(c == 1)
                def _():
                    piece_here(i).wait()

                @pl.when(c == 0)
                def _():
                    piece_over(i, other).wait_recv()

            cosine = by_lanes(wunit[...].astype(BF16), rows_of(side, i))
            hit = column_ref[...] == labels_ref[pl.ds(side * pieces + i, 1)]
            value = jnp.exp(logit_scale * jnp.where(hit, cosine - margin, cosine))
            expo[side * pieces + i] = value
            den[group, 0, pl.ds(2 * (i - 4 * group) + side, 1)] = jnp.sum(value, axis=0, keepdims=True)

    stages = ((0, [partner]), (1, along_x), (4, along_y), (7, along_z))

    def stage_copies(group, stage):
        slot, peers = stages[stage]
        return [
            remote(
                den.at[group, stage],
                got.at[group, slot + k],
                den_sent.at[10 * group + slot + k],
                den_came.at[10 * group + slot + k],
                peer,
            )
            for k, peer in enumerate(peers)
        ]

    def stage_start(group, stage):
        for copy in stage_copies(group, stage):
            copy.start()

    def stage_end(group, stage):
        for copy in stage_copies(group, stage):
            copy.wait()
        slot, peers = stages[stage]
        total = den[group, stage]
        for k in range(len(peers)):
            total = total + got[group, slot + k]
        if stage < 3:
            den[group, stage + 1] = total
            stage_start(group, stage + 1)
        else:
            inverse[group] = logit_scale / total

    def gradients(group, i):
        for side in range(2):
            b = side * pieces + i
            hit = column_ref[...] == labels_ref[pl.ds(b, 1)]
            share = expo[b] * inverse[group, pl.ds(2 * (i - 4 * group) + side, 1)]
            grad = jnp.where(hit, share - logit_scale, share).astype(BF16)
            expo[b] = grad.astype(F32)
            acc[...] += jnp.dot(grad, rows_of(side, i), preferred_element_type=F32)

    acc[...] = jnp.zeros_like(acc)

    @pl.loop(0, 4)
    def _(i):
        exponents(0, i)

    stage_start(0, 0)
    for n in range(4):
        exponents(1, 4 + n)
        if n == 3:
            stage_start(1, 0)
        stage_end(0, n)
    for n in range(4):
        gradients(0, n)
        stage_end(1, n)

    @pl.loop(4, pieces)
    def _(i):
        gradients(1, i)

    dwhat = acc[...]
    unit = wunit[...]
    _, col_norm = column_norm()
    dfetched = ((dwhat - unit * jnp.sum(unit * dwhat, axis=1, keepdims=True)) / col_norm).astype(BF16)
    kept = dfetched.shape[0]
    place = flag(slot_ref[...] == iota((N_TILES * slots, kept), 0)).astype(BF16)
    packed[...] = jnp.dot(place, dfetched, preferred_element_type=F32).astype(BF16).reshape(packed.shape)

    def give(t):
        return remote(packed.at[t], arrived.at[me], row_sent.at[t], row_came.at[me], tile_device(z, t))

    def given(t):
        return remote(packed.at[t], arrived.at[t], row_sent.at[t], row_came.at[t], tile_device(z, t))

    @pl.loop(1, N_TILES)
    def _(k):
        give(lax.rem(me + k, N_TILES)).start()

    arrived[me] = packed[me]

    def tiles_of(n):
        return pl.ds(8 * ahead(y, n), 8)

    def down(n):
        return remote(
            arrived.at[tiles_of(n)], nearby.at[0, tiles_of(n)], ring_sent.at[n], ring_came.at[n], along_z[2]
        )

    def up(n):
        return remote(
            arrived.at[tiles_of(n)], nearby.at[1, tiles_of(n)], ring_sent.at[4 + n], ring_came.at[4 + n], along_z[0]
        )

    def onward(n):
        source, device = (1, along_z[0]) if n < 2 else (0, along_z[2])
        return remote(
            nearby.at[source, tiles_of(n)],
            nearby.at[2, tiles_of(n)],
            ring_sent.at[8 + n],
            ring_came.at[8 + n],
            device,
        )

    def pass_on(n):
        for j in range(8):
            t = 8 * ahead(y, n) + j
            if n:
                given(t).wait_recv()
            else:

                @pl.when(t != me)
                def _(t=t):
                    given(t).wait_recv()

        up(n).start()
        down(n).start()

    half = mine.shape[2] // 2
    low, high = pl.ds(0, half), pl.ds(half, half)

    def product(side, i):
        return jnp.dot(turned[...], expo[side * pieces + i].astype(BF16), preferred_element_type=F32)

    def hand_over(i):
        two = pl.ds(2 * i, 2)
        return remote(over.at[two], came.at[two], over_sent.at[i], over_came.at[i], partner)

    @pl.loop(0, pieces)
    def _(i):
        part = product(other, i).astype(BF16)
        over[2 * i] = part[:, : part.shape[1] // 2]
        over[2 * i + 1] = part[:, part.shape[1] // 2 :]
        hand_over(i).start()

    def own_part(i):
        part = product(c, i)
        hand_over(i).wait_recv()
        lanes = part.shape[1] // 2
        row, column = lax.div(i, 2), 2 * lax.rem(i, 2)
        mine[row, column] = (part[:, :lanes] + came[2 * i].astype(F32)).astype(BF16)
        mine[row, column + 1] = (part[:, lanes:] + came[2 * i + 1].astype(F32)).astype(BF16)

    pass_on(0)
    pl.loop(0, 4)(own_part)
    pass_on(1)
    pl.loop(4, 8)(own_part)
    pass_on(2)
    pass_on(3)

    def step(n, src, dst, device):
        return remote(src, dst, step_sent.at[n], step_came.at[n], device)

    one_a = [step(k, mine.at[:, ahead(x, k + 1), low], first_a.at[k], along_x[k]) for k in others]
    one_b = [step(3 + k, mine.at[ahead(y, k + 1), :, high], first_b.at[k], along_y[k]) for k in others]
    for copy in one_a + one_b:
        copy.start()

    block = expo.shape[1]

    def scatter(source, rows_ref, fresh):
        slot_rows = rows_ref.reshape(N_TILES * slots, rows_ref.shape[2])
        index = index_ref[source]

        @pl.loop(0, pieces)
        def _(r):
            pick = flag(iota((block, N_TILES * slots), 0) + r * block == index).astype(BF16)
            grad = jnp.dot(pick, slot_rows, preferred_element_type=F32)
            expo[r] = grad if fresh else expo[r] + grad

    scatter(z, arrived[...], True)
    for n in range(2):
        up(n).wait_recv()
        onward(n).start()
    for n in range(2, 4):
        down(n).wait_recv()
        onward(n).start()
    for n in range(2):
        down(n).wait_recv()
    scatter(ahead(z, 1), nearby[0], False)
    for n in range(2, 4):
        up(n).wait_recv()
    scatter(ahead(z, 3), nearby[1], False)
    for copy in one_a + one_b:
        copy.wait_recv()

    @pl.loop(0, ACROSS)
    def _(i):
        total, below = mine[i, x, low].astype(F32), mine[y, i, high].astype(F32)
        for k in others:
            total = total + first_a[k, i].astype(F32)
            below = below + first_b[k, i].astype(F32)
        next_a[i] = total.astype(BF16)
        next_b[i] = below.astype(BF16)

    two_a = [step(6 + k, next_a.at[ahead(y, k + 1)], second_a.at[k], along_y[k]) for k in others]
    two_b = [step(9 + k, next_b.at[ahead(x, k + 1)], second_b.at[k], along_x[k]) for k in others]
    for copy in two_a + two_b:
        copy.start()
    for n in range(4):
        onward(n).wait_recv()
    scatter(ahead(z, 2), nearby[2], False)
    save = [pltpu.make_async_copy(expo.at[pl.ds(0, pieces)], grads_hbm, out_sem.at[0])]
    save[0].start()
    for copy in two_a + two_b:
        copy.wait_recv()
    top, bottom = next_a[y].astype(F32), next_b[x].astype(F32)
    for k in others:
        top = top + second_a[k].astype(F32)
        bottom = bottom + second_b[k].astype(F32)
    rows = last.shape[1]
    last[:, :, :half] = top.T.astype(BF16).reshape(ACROSS, rows, half)
    last[:, :, half:] = bottom.T.astype(BF16).reshape(ACROSS, rows, half)
    three = [step(12 + k, last.at[ahead(z, k + 1)], third.at[k], along_z[k]) for k in others]
    for copy in three:
        copy.start()
    xfloat = emb_ref[...].astype(F32)
    row_norm = jnp.sqrt(jnp.sum(xfloat * xfloat, axis=1, keepdims=True) + eps)
    xunit = xfloat / row_norm
    for copy in three:
        copy.wait_recv()
    dunit = last[z].astype(F32)
    for k in others:
        dunit = dunit + third[k].astype(F32)
    emb_out[...] = (dunit - xunit * jnp.sum(xunit * dunit, axis=1, keepdims=True)) / row_norm
    for copy in one_a + one_b + two_a + two_b + three:
        copy.wait_send()
    for n in range(4):
        up(n).wait_send()
        down(n).wait_send()
        onward(n).wait_send()

    @pl.loop(0, pieces)
    def _(i):
        hand_over(i).wait_send()
        piece_over(i, c).wait_send()

    @pl.loop(1, N_TILES)
    def _(k):
        give(lax.rem(me + k, N_TILES)).wait_send()

    save[0].wait()


def margin_step(xhalf, fetched, labels, column, slot, index, embeddings, slots, homes):
    kept, width = fetched.shape
    blocks, block = labels.shape
    rows = embeddings.shape[0]
    half, lanes = width // 2, block // 2
    vmem, anywhere = pl.BlockSpec(memory_space=pltpu.VMEM), pl.BlockSpec(memory_space=pl.ANY)
    return pl.pallas_call(
        margin_kernel,
        in_specs=[anywhere] + [vmem] * 6,
        out_specs=[anywhere, vmem],
        out_shape=[
            jax.ShapeDtypeStruct((homes // block, block, width), F32),
            jax.ShapeDtypeStruct((rows, width), F32),
        ],
        scratch_shapes=[
            pltpu.VMEM((2, *xhalf.shape), BF16),
            pltpu.VMEM((blocks, kept, block), F32),
            pltpu.VMEM((2, 4, blocks // 2, block), F32),
            pltpu.VMEM((2, 10, blocks // 2, block), F32),
            pltpu.VMEM((2, blocks // 2, block), F32),
            pltpu.VMEM((kept, width), F32),
            pltpu.VMEM((kept, width), F32),
            pltpu.VMEM((width, kept), BF16),
            pltpu.VMEM((N_TILES, slots, width), BF16),
            pltpu.VMEM((N_TILES, slots, width), BF16),
            pltpu.VMEM((3, N_TILES, slots, width), BF16),
            pltpu.VMEM((blocks, width, lanes), BF16),
            pltpu.VMEM((blocks, width, lanes), BF16),
            pltpu.VMEM((ACROSS, ACROSS, width, lanes), BF16),
            pltpu.VMEM((3, ACROSS, half, lanes), BF16),
            pltpu.VMEM((3, ACROSS, half, lanes), BF16),
            pltpu.VMEM((ACROSS, half, lanes), BF16),
            pltpu.VMEM((ACROSS, half, lanes), BF16),
            pltpu.VMEM((3, half, lanes), BF16),
            pltpu.VMEM((3, half, lanes), BF16),
            pltpu.VMEM((ACROSS, rows, width), BF16),
            pltpu.VMEM((3, rows, width), BF16),
        ]
        + [pltpu.SemaphoreType.DMA((8,))] * 3
        + [pltpu.SemaphoreType.DMA((20,))] * 2
        + [pltpu.SemaphoreType.DMA((N_TILES,))] * 2
        + [pltpu.SemaphoreType.DMA((12,))] * 2
        + [pltpu.SemaphoreType.DMA((8,))] * 2
        + [pltpu.SemaphoreType.DMA((15,))] * 2
        + [pltpu.SemaphoreType.DMA((1,))],
        compiler_params=pltpu.CompilerParams(
            collective_id=1, has_side_effects=True, vmem_limit_bytes=60 * 2**20
        ),
        name="margin_step",
    )(xhalf, fetched, labels, column, slot, index, embeddings)


def body(embeddings, labels, centres, momentum, sample_home, sample_row):
    groups = lax.axis_size("dp")
    tile = lax.axis_index(CLS)
    columns = sample_row.shape[0]
    kept = columns // groups
    slots = 2 * kept // N_TILES
    rows, width = embeddings.shape
    homes = centres.shape[0]
    xhalf, fetched, column, slot, index, labels = fetch(
        embeddings,
        sample_home.reshape(1, columns),
        sample_row.reshape(1, columns),
        labels.reshape(16, 128),
        centres,
        kept,
        slots,
    )
    labels = labels.reshape(groups, 16, 2, rows).transpose(2, 1, 0, 3).reshape(16, -1) - tile * columns
    index = index[:, :, 0, :slots].reshape(groups, 1, N_TILES * slots)
    centre_grad, emb_grad = margin_step(
        xhalf.reshape(groups, 16, rows, width), fetched, labels, column, slot, index, embeddings, slots, homes
    )
    centre_float = centres.astype(F32)
    momentum_new = momentum_rate * momentum + centre_grad.reshape(homes, width) + weight_decay * centre_float
    centres_new = (centre_float - learn_rate * momentum_new).astype(BF16)
    return (emb_grad, momentum_new, centres_new)


def solution(mesh):
    torus = Mesh(mesh.devices.reshape(mesh.shape["dp"], 4, 4, 2), ("dp", "cls_0", "cls_1", "cls_2"))
    return jax.shard_map(
        body,
        mesh=torus,
        in_specs=(P(DP_CLS, None), P("dp"), P(CLS, None), P(CLS, None), P(CLS, None), P(CLS)),
        out_specs=(P(DP_CLS, None), P(CLS, None), P(CLS, None)),
        check_vma=False,
    )
```

```python
import jax
import jax.numpy as jnp
from jax import lax
from jax.experimental import pallas as pl
from jax.experimental.pallas import tpu as pltpu
from jax.sharding import Mesh
from jax.sharding import PartitionSpec as P

CLS = ("cls_0", "cls_1", "cls_2")
DP_CLS = ("dp", "cls_0", "cls_1", "cls_2")

eps = 1e-06
logit_scale = 64.0
margin = 0.35
momentum_rate = 0.9
learn_rate = 0.1
weight_decay = 0.0005
BF16 = jnp.bfloat16
F32 = jnp.float32


MESH = pl.DeviceIdType.MESH
N_TILES = 32
ACROSS = 4


def where_am_i():
    z, y, x, c = (lax.axis_index(name) for name in DP_CLS)
    return z, y, x, c, y * 8 + x * 2 + c


def ahead(position, k):
    return lax.rem(position + k, ACROSS)


def tile_device(z, t):
    return (z, lax.div(t, 8), lax.rem(lax.div(t, 2), ACROSS), lax.rem(t, 2))


def remote(src, dst, send, recv, device):
    return pltpu.make_async_remote_copy(
        src_ref=src, dst_ref=dst, send_sem=send, recv_sem=recv, device_id=device, device_id_type=MESH
    )


def greet(devices, tiles=None):
    barrier = pltpu.get_barrier_semaphore()
    for device in devices:
        pl.semaphore_signal(barrier, inc=1, device_id=device, device_id_type=MESH)
    count = len(devices)
    if tiles is not None:
        z, me = tiles

        @pl.loop(1, N_TILES)
        def _(k):
            pl.semaphore_signal(
                barrier, inc=1, device_id=tile_device(z, lax.rem(me + k, N_TILES)), device_id_type=MESH
            )

        count += N_TILES - 1
    return barrier, count


def by_lanes(a, b):
    return lax.dot_general(a, b, (((1,), (1,)), ((), ())), preferred_element_type=F32)


def flag(condition):
    return jnp.where(condition, 1.0, 0.0)


def iota(shape, dim):
    return lax.broadcasted_iota(jnp.int32, shape, dim)


def plan_request(home, row, group):
    columns = home.shape[1]
    block = 128
    cuts = [slice(b * block, (b + 1) * block) for b in range(columns // block)]
    at_home = flag(iota((N_TILES, columns), 0) == home)
    upper = flag(iota((block, block), 0) < iota((block, block), 1)).astype(BF16)
    stacked = jnp.concatenate([at_home[:, cut] for cut in cuts], axis=0).astype(BF16)
    within = jnp.dot(stacked, upper, preferred_element_type=F32)
    before = [jnp.zeros((N_TILES, 1), F32)]
    for cut in cuts:
        before.append(before[-1] + jnp.sum(at_home[:, cut], axis=1, keepdims=True))
    count = jnp.broadcast_to(before[-1], (N_TILES, block)).astype(BF16)
    lower = flag(iota((N_TILES, N_TILES), 1) < iota((N_TILES, N_TILES), 0)).astype(BF16)
    offset = jnp.dot(lower, count, preferred_element_type=F32)
    first = ((offset.astype(jnp.int32) + (ACROSS - 1 - group)) >> 2).astype(F32)
    places, starts = [], []
    for b, cut in enumerate(cuts):
        mark = at_home[:, cut]
        rank = within[b * N_TILES : (b + 1) * N_TILES] + before[b] + offset
        places.append(jnp.sum(mark * rank, axis=0, keepdims=True))
        starts.append(jnp.sum(mark * first, axis=0, keepdims=True))
    place = jnp.concatenate(places, axis=1).astype(jnp.int32)
    start = jnp.concatenate(starts, axis=1).astype(jnp.int32)
    mine = (place & 3) == group
    kept = place >> 2
    slot = kept - start
    by_slot = flag(mine & (iota((block, columns), 0) == slot)).astype(BF16)
    digits = [at_home * (row >> 6).astype(F32), at_home * (row & 63).astype(F32)]
    asked = by_lanes(jnp.concatenate(digits, axis=0).astype(BF16), by_slot)
    return (asked[:N_TILES] * 64 + asked[N_TILES:]).astype(jnp.int32), mine, kept, slot


def plan_kept(home, mine, kept, slot, slots):
    columns, block = home.shape[1], 128
    by_kept = flag(mine & (iota((block, columns), 0) == (kept & 127))).astype(BF16)
    lane = iota((1, columns), 1)
    parts = []
    for value in (home, slot, lane >> 6, lane & 63):
        for a in range(ACROSS):
            parts.append(jnp.where((kept >> 7) == a, value.astype(F32), 0.0))
    found = by_lanes(jnp.concatenate(parts, axis=0).astype(BF16), by_kept)
    turned = jnp.concatenate([found, jnp.zeros((block - found.shape[0], block), F32)], axis=0).T
    runs = range(ACROSS)
    slot_row = jnp.concatenate([found[a : a + 1] * slots + found[4 + a : 5 + a] for a in runs], axis=1)
    slot_column = jnp.concatenate([turned[:, a : a + 1] * slots + turned[:, 4 + a : 5 + a] for a in runs], axis=0)
    column = jnp.concatenate([turned[:, 8 + a : 9 + a] * 64 + turned[:, 12 + a : 13 + a] for a in runs], axis=0)
    return slot_row.astype(jnp.int32), slot_column.astype(jnp.int32), column.astype(jnp.int32)


def step_kernel(
    emb_hbm, home_hbm, row_hbm, labels_hbm, centres_hbm, momentum_hbm, momentum_out, emb_out,
    emb, home, row, labels_here, labels_all, labels_at, labels, request, incoming, index_all, index,
    column, slot_row, xall, expo, den, got, inverse, acc, fetched, wunit, scaled, turned, replies, replied, packed, arrived,
    nearby, over, came, mine, first_a, first_b, next_a, next_b, second_a, second_b, last, third,
    local_sem, request_sent, request_came, reply_sent, reply_came, tell_sent, tell_came, phase_sent, phase_came,
    x_sent, x_came, den_sent, den_came, row_sent, row_came, ring_sent, ring_came, over_sent, over_came,
    step_sent, step_came,
):
    z, y, x, c, me = where_am_i()
    other = 1 - c
    partner = (z, y, x, other)
    others = range(ACROSS - 1)
    along_x = [(z, y, ahead(x, k + 1), c) for k in others]
    along_y = [(z, ahead(y, k + 1), x, c) for k in others]
    along_z = [(ahead(z, k + 1), y, x, c) for k in others]
    along = {"x": along_x, "y": along_y, "z": along_z}
    pieces = 8
    slots = packed.shape[1]
    block, width = expo.shape[1], expo.shape[2]
    kept = block
    lanes = width // 2

    def local(src, dst, n):
        return pltpu.make_async_copy(src, dst, local_sem.at[n])

    def load_centres(i):
        rows, columns = pl.ds(block * (i // 2), block), pl.ds(lanes * (i % 2), lanes)
        return local(centres_hbm.at[rows, columns], over.at[i], 8 + i)

    small = [
        local(src, dst, n)
        for n, (src, dst) in enumerate(
            ((home_hbm, home), (row_hbm, row), (emb_hbm, emb), (labels_hbm, labels_here))
        )
    ]
    for copy in small:
        copy.start()
    for i in range(2 * pieces):
        load_centres(i).start()
    barrier, count = greet(along_z, (z, me))
    for copy in small:
        copy.wait()
    xfloat = emb[...].astype(F32)
    row_norm = jnp.sqrt(jnp.sum(xfloat * xfloat, axis=1, keepdims=True) + eps)
    xall[c, z, y, x] = (xfloat / row_norm).astype(BF16)

    def ask(k):
        t = lax.rem(me + k, N_TILES)
        return remote(request.at[t], incoming.at[me], request_sent.at[t], request_came.at[me], tile_device(z, t))

    def asked_by(t):
        return remote(request.at[t], incoming.at[t], request_sent.at[t], request_came.at[t], tile_device(z, t))

    def answer(t):
        return remote(replies.at[t], replied.at[me], reply_sent.at[t], reply_came.at[me], tile_device(z, t))

    def answered(t):
        return remote(replies.at[t], replied.at[t], reply_sent.at[t], reply_came.at[t], tile_device(z, t))

    parts = ((0, 16, "zxy"), (16, 16, "zyx"), (32, 32, "xyz"))
    place = {"z": z, "y": y, "x": x}

    def held(part, phase, position, cut=None):
        first, size, axes = parts[part]
        at = dict(place)
        for n in range(phase):
            at[axes[n]] = pl.ds(0, ACROSS)
        if cut is not None:
            at[axes[0]] = pl.ds(2 * cut, 2)
        at[axes[phase]] = position
        return xall.at[c, at["z"], at["y"], at["x"], pl.ds(first, size)]

    def spread(part, phase, kind):
        axis = parts[part][2][phase]
        position, peers = place[axis], along[axis]
        n = 4 * (3 * part + phase)

        def one(k, ref, peer):
            return remote(ref, ref, phase_sent.at[n + k], phase_came.at[n + k], peers[peer])

        if phase == 0:
            mine_here = held(part, phase, position)
            return [one(k, mine_here, k) for k in others] if kind == 0 else []
        if kind == 0:
            mine_here = held(part, phase, position)
            return [one(0, mine_here, 0), one(1, mine_here, 2)]
        return [
            one(2, held(part, phase, ahead(position, 3), 0), 0),
            one(3, held(part, phase, ahead(position, 1), 1), 2),
        ]

    flying = []

    def send(copies):
        for copy in copies:
            copy.start()
        flying.extend(copies)

    def land(copies):
        for copy in copies:
            copy.wait_recv()

    tell = [
        remote(labels_here, labels_all.at[k], tell_sent.at[k], tell_came.at[k], along_z[k]) for k in others
    ]
    pl.semaphore_wait(barrier, count)
    for part in (2, 0, 1):
        send(spread(part, 0, 0))
    asked, taken, kept_as, slot_at = plan_request(home[...], row[...], z)
    request[...] = asked.reshape(request.shape)

    @pl.loop(1, N_TILES)
    def _(k):
        ask(k).start()

    send(tell)
    incoming[me] = request[me]
    for part in (2, 0, 1):
        land(spread(part, 0, 0))
        send(spread(part, 1, 0))
    slot_row[...], slot_column, column[...] = plan_kept(home[...], taken, kept_as, slot_at, slots)
    for part in (2, 0, 1):
        land(spread(part, 1, 0))
        send(spread(part, 1, 1))

    @pl.loop(1, N_TILES)
    def _(k):
        asked_by(lax.rem(me + k, N_TILES)).wait_recv()

    share = [
        remote(incoming, index_all.at[k], tell_sent.at[3 + k], tell_came.at[3 + k], along_z[k]) for k in others
    ]
    send(share)
    for i in range(2 * pieces):
        load_centres(i).wait()
    row_ids = iota((slots, pieces * block), 1)
    for turn, q in enumerate((1, 2, 3, 0)):
        first = ahead(y, q) * 8
        wanted = incoming[pl.ds(first, 8)].reshape(8, 128).T
        pick = jnp.concatenate(
            [flag(row_ids == wanted[:slots, j : j + 1]).astype(BF16) for j in range(8)], axis=0
        )
        found = []
        for h in range(2):
            half_found = jnp.zeros((8 * slots, lanes), F32)
            for r in range(pieces):
                half_found += jnp.dot(
                    pick[:, r * block : (r + 1) * block], over[2 * r + h], preferred_element_type=F32
                )
            found.append(half_found.astype(BF16))
        replies[pl.ds(first, 8)] = jnp.concatenate(found, axis=1).reshape(8, slots, width)
        for j in range(8):
            if q:
                answer(first + j).start()
            else:

                @pl.when(first + j != me)
                def _(t=first + j):
                    answer(t).start()

        if turn == 0:
            for part in (2, 0, 1):
                land(spread(part, 1, 1))
                send(spread(part, 2, 0))

    replied[me] = replies[me]
    land(tell + share)
    labels_at[z] = labels_here[...]
    for k in others:
        labels_at[ahead(z, 3 - k)] = labels_all[k]
    rows = emb.shape[0]
    for side in range(2):
        for i in range(pieces):
            runs = [
                labels_at[g, 2 * i + j : 2 * i + j + 1, side * rows : (side + 1) * rows]
                for j in range(2)
                for g in range(ACROSS)
            ]
            labels[side * pieces + i : side * pieces + i + 1] = (
                jnp.concatenate(runs, axis=1) - me * home.shape[1]
            )

    def along_lanes(ref):
        return jnp.concatenate([ref[t][:, :slots] for t in range(N_TILES)], axis=1)

    index[0] = along_lanes(incoming)
    for n, k in ((1, 2), (2, 0), (3, 1)):
        index[n] = along_lanes(index_all.at[k])
    for part in (0, 1, 2):
        land(spread(part, 2, 0))
        send(spread(part, 2, 1))

    @pl.loop(1, N_TILES)
    def _(k):
        answered(lax.rem(me + k, N_TILES)).wait_recv()

    pick = flag(slot_column == iota((kept, N_TILES * slots), 1)).astype(BF16)
    wfloat = jnp.dot(pick, replied[...].reshape(N_TILES * slots, width), preferred_element_type=F32)
    fetched[...] = wfloat.astype(BF16)
    col_norm = jnp.sqrt(jnp.sum(wfloat * wfloat, axis=1, keepdims=True) + eps)
    wunit[...] = wfloat / col_norm
    scaled[...] = (logit_scale * wunit[...]).astype(BF16)
    turned[...] = wunit[...].T.astype(BF16)

    def swap_part(part, slot):
        first, size, _ = parts[part]
        ref = xall.at[slot, :, :, :, pl.ds(first, size)]
        return remote(ref, ref, x_sent.at[pieces + part], x_came.at[pieces + part], partner)

    def swap_piece(i, slot):
        first, size, _ = parts[2]
        ref = xall.at[slot, :, lax.div(i, 2), pl.ds(2 * lax.rem(i, 2), 2), pl.ds(first, size)]
        return remote(ref, ref, x_sent.at[i], x_came.at[i], partner)

    for part in (0, 1):
        land(spread(part, 2, 1))
        swap_part(part, c).start()
    land(spread(2, 2, 1))

    @pl.loop(0, pieces)
    def _(i):
        swap_piece(i, c).start()

    for part in (0, 1):
        swap_part(part, other).wait_recv()

    def rows_of(side, i):
        y_of, x_of = lax.div(i, 2), 2 * lax.rem(i, 2)
        return jnp.concatenate(
            [xall[side, g, y_of, x_of + j] for j in range(2) for g in range(ACROSS)], axis=0
        )

    def exponents(group, i):
        swap_piece(i, other).wait_recv()
        for side in range(2):
            logit = by_lanes(scaled[...], rows_of(side, i))
            hit = column[...] == labels[pl.ds(side * pieces + i, 1)]
            value = jnp.exp(jnp.where(hit, logit - logit_scale * margin, logit))
            expo[side * pieces + i] = value
            den[group, 0, pl.ds(2 * (i - 4 * group) + side, 1)] = jnp.sum(value, axis=0, keepdims=True)

    stages = ((0, [partner]), (1, along_x), (4, along_y), (7, along_z))

    def stage_copies(group, stage):
        slot, peers = stages[stage]
        return [
            remote(
                den.at[group, stage],
                got.at[group, slot + k],
                den_sent.at[10 * group + slot + k],
                den_came.at[10 * group + slot + k],
                peer,
            )
            for k, peer in enumerate(peers)
        ]

    def stage_start(group, stage):
        for copy in stage_copies(group, stage):
            copy.start()

    def stage_end(group, stage):
        for copy in stage_copies(group, stage):
            copy.wait()
        slot, peers = stages[stage]
        total = den[group, stage]
        for k in range(len(peers)):
            total = total + got[group, slot + k]
        if stage < 3:
            den[group, stage + 1] = total
            stage_start(group, stage + 1)
        else:
            inverse[group] = logit_scale / total

    def gradients(group, i):
        for side in range(2):
            b = side * pieces + i
            hit = column[...] == labels[pl.ds(b, 1)]
            share = expo[b] * inverse[group, pl.ds(2 * (i - 4 * group) + side, 1)]
            grad = jnp.where(hit, share - logit_scale, share).astype(BF16)
            expo[b] = grad.astype(F32)
            acc[...] += jnp.dot(grad, rows_of(side, i), preferred_element_type=F32)

    half = mine.shape[2] // 2
    low, high = pl.ds(0, half), pl.ds(half, half)

    def product(side, i):
        return jnp.dot(turned[...], expo[side * pieces + i].astype(BF16), preferred_element_type=F32)

    def hand_over(i):
        two = pl.ds(2 * i, 2)
        return remote(over.at[two], came.at[two], over_sent.at[i], over_came.at[i], partner)

    def give_over(i):
        part = product(other, i).astype(BF16)
        over[2 * i] = part[:, :lanes]
        over[2 * i + 1] = part[:, lanes:]
        hand_over(i).start()

    def own_part(i):
        part = product(c, i)
        hand_over(i).wait_recv()
        y_of, x_of = lax.div(i, 2), 2 * lax.rem(i, 2)
        mine[y_of, x_of] = (part[:, :lanes] + came[2 * i].astype(F32)).astype(BF16)
        mine[y_of, x_of + 1] = (part[:, lanes:] + came[2 * i + 1].astype(F32)).astype(BF16)

    acc[...] = jnp.zeros_like(acc)

    @pl.loop(0, 4)
    def _(i):
        exponents(0, i)

    stage_start(0, 0)
    for n in range(4):
        exponents(1, 4 + n)
        if n == 3:
            stage_start(1, 0)
        stage_end(0, n)
    for n in range(4):
        gradients(0, n)
        give_over(n)
        if n:
            own_part(n - 1)
        stage_end(1, n)
    own_part(3)

    @pl.loop(4, pieces)
    def _(i):
        gradients(1, i)

    dwhat = acc[...]
    unit = wunit[...]
    wfloat = fetched[...].astype(F32)
    col_norm = jnp.sqrt(jnp.sum(wfloat * wfloat, axis=1, keepdims=True) + eps)
    dfetched = ((dwhat - unit * jnp.sum(unit * dwhat, axis=1, keepdims=True)) / col_norm).astype(BF16)
    pick = flag(slot_row[...] == iota((N_TILES * slots, kept), 0)).astype(BF16)
    packed[...] = jnp.dot(pick, dfetched, preferred_element_type=F32).astype(BF16).reshape(packed.shape)

    def give(t):
        return remote(packed.at[t], arrived.at[me], row_sent.at[t], row_came.at[me], tile_device(z, t))

    def given(t):
        return remote(packed.at[t], arrived.at[t], row_sent.at[t], row_came.at[t], tile_device(z, t))

    for q in range(ACROSS):
        for j in range(8):
            if q:
                give(8 * ahead(y, q) + j).start()
            else:

                @pl.when(8 * y + j != me)
                def _(t=8 * y + j):
                    give(t).start()

    arrived[me] = packed[me]

    def tiles_of(n):
        return pl.ds(8 * ahead(y, (ACROSS - n) % ACROSS), 8)

    def down(n):
        return remote(
            arrived.at[tiles_of(n)], nearby.at[0, tiles_of(n)], ring_sent.at[n], ring_came.at[n], along_z[2]
        )

    def up(n):
        return remote(
            arrived.at[tiles_of(n)], nearby.at[1, tiles_of(n)], ring_sent.at[4 + n], ring_came.at[4 + n], along_z[0]
        )

    def onward(n):
        source, device = (1, along_z[0]) if n < 2 else (0, along_z[2])
        return remote(
            nearby.at[source, tiles_of(n)],
            nearby.at[2, tiles_of(n)],
            ring_sent.at[8 + n],
            ring_came.at[8 + n],
            device,
        )

    def pass_on(n):
        for j in range(8):
            t = 8 * ahead(y, (ACROSS - n) % ACROSS) + j
            if n:
                given(t).wait_recv()
            else:

                @pl.when(t != me)
                def _(t=t):
                    given(t).wait_recv()

        up(n).start()
        down(n).start()

    pl.loop(4, 8)(give_over)
    pass_on(0)
    pl.loop(4, 8)(own_part)
    pass_on(1)

    def sum_over(n, position, peers, part, inbox):
        up_at, far_at, down_at = (ahead(position, k) for k in (1, 2, 3))

        def hop(k, src, dst, device):
            return remote(src, dst, step_sent.at[n + k], step_came.at[n + k], device)

        early = [
            hop(0, part(far_at, 0), inbox.at[2, 0], peers[0]),
            hop(1, part(far_at, 1), inbox.at[2, 1], peers[2]),
            hop(2, part(up_at, 1), inbox.at[0, 1], peers[0]),
            hop(3, part(down_at, 0), inbox.at[1, 0], peers[2]),
        ]
        late = [hop(4, part(up_at, 0), inbox.at[0, 0], peers[0]), hop(5, part(down_at, 1), inbox.at[1, 1], peers[2])]
        for copy in early:
            copy.start()

        def relay():
            for k, ref in ((0, part(up_at, 0)), (1, part(down_at, 1))):
                early[k].wait_recv()
                ref[...] = (ref[...].astype(F32) + inbox[2, k].astype(F32)).astype(BF16)
                late[k].start()
            flying.extend(early + late)

        return relay, early[2:] + late

    relay_a, rest_a = sum_over(0, x, along_x, lambda p, h: mine.at[pl.ds(2 * h, 2), p, low], first_a)
    relay_b, rest_b = sum_over(6, y, along_y, lambda p, h: mine.at[p, pl.ds(2 * h, 2), high], first_b)

    pass_on(2)
    pass_on(3)

    @pl.loop(0, pieces)
    def _(i):
        hand_over(i).wait_send()

    old = local(momentum_hbm, expo.at[pl.ds(pieces, pieces)], 4)
    old.start()
    for i in range(2 * pieces):
        load_centres(i).start()
    old.wait()
    for i in range(2 * pieces):
        load_centres(i).wait()

    def save(r):
        return local(expo.at[r], momentum_out.at[r], 8 + r)

    def scatter(n, rows_ref, fresh=False, final=False):
        slot_rows = rows_ref.reshape(N_TILES * slots, width)
        wanted = index[n]

        @pl.loop(0, pieces)
        def _(r):
            pick = flag(iota((block, N_TILES * slots), 0) + r * block == wanted).astype(BF16)
            grad = jnp.dot(pick, slot_rows, preferred_element_type=F32)
            if fresh:
                centre = jnp.concatenate([over[2 * r], over[2 * r + 1]], axis=1).astype(F32)
                grad = momentum_rate * expo[pieces + r] + grad + weight_decay * centre
                expo[r] = grad
            else:
                expo[r] = expo[r] + grad
            if final:
                save(r).start()

    for n in range(2):
        up(n).wait_recv()
        onward(n).start()
    scatter(0, arrived[...], fresh=True)
    relay_a()
    relay_b()
    down(2).wait_recv()
    onward(2).start()
    land(rest_a + rest_b)

    @pl.loop(0, ACROSS)
    def _(i):
        h, j = lax.div(i, 2), lax.rem(i, 2)
        total, below = mine[i, x, low].astype(F32), mine[y, i, high].astype(F32)
        for k in range(2):
            total = total + first_a[k, h, j].astype(F32)
            below = below + first_b[k, h, j].astype(F32)
        next_a[i] = total.astype(BF16)
        next_b[i] = below.astype(BF16)

    quarter = half // 2
    relay_a, rest_a = sum_over(12, y, along_y, lambda p, h: next_a.at[p, pl.ds(quarter * h, quarter)], second_a)
    relay_b, rest_b = sum_over(18, x, along_x, lambda p, h: next_b.at[p, pl.ds(quarter * h, quarter)], second_b)
    down(3).wait_recv()
    onward(3).start()
    relay_a()
    relay_b()
    for n in range(2):
        down(n).wait_recv()
    scatter(1, nearby[0])
    for n in range(2, 4):
        up(n).wait_recv()
    scatter(2, nearby[1])
    land(rest_a + rest_b)
    top, bottom = next_a[y].astype(F32), next_b[x].astype(F32)
    for k in range(2):
        top = top + second_a[k].astype(F32).reshape(half, lanes)
        bottom = bottom + second_b[k].astype(F32).reshape(half, lanes)
    last[:, :, :half] = top.T.astype(BF16).reshape(ACROSS, rows, half)
    last[:, :, half:] = bottom.T.astype(BF16).reshape(ACROSS, rows, half)
    three = [
        remote(last.at[ahead(z, k + 1)], third.at[k], step_sent.at[24 + k], step_came.at[24 + k], along_z[k])
        for k in others
    ]
    send(three)
    land([onward(n) for n in range(4)])
    scatter(3, nearby[2], final=True)
    xfloat = emb[...].astype(F32)
    row_norm = jnp.sqrt(jnp.sum(xfloat * xfloat, axis=1, keepdims=True) + eps)
    xunit = xfloat / row_norm
    land(three)
    dunit = last[z].astype(F32)
    for k in others:
        dunit = dunit + third[k].astype(F32)
    emb_out[...] = (dunit - xunit * jnp.sum(xunit * dunit, axis=1, keepdims=True)) / row_norm
    for copy in flying:
        copy.wait_send()
    for n in range(4):
        up(n).wait_send()
        down(n).wait_send()
        onward(n).wait_send()
    for part in (0, 1):
        swap_part(part, c).wait_send()

    @pl.loop(0, pieces)
    def _(i):
        swap_piece(i, c).wait_send()

    @pl.loop(1, N_TILES)
    def _(k):
        ask(k).wait_send()
        answer(lax.rem(me + k, N_TILES)).wait_send()
        give(lax.rem(me + k, N_TILES)).wait_send()

    @pl.loop(0, pieces)
    def _(r):
        save(r).wait()


def step(embeddings, home, row, labels, centres, momentum):
    rows, width = embeddings.shape
    columns = home.shape[1]
    homes = centres.shape[0]
    kept = columns // ACROSS
    slots = 2 * kept // N_TILES
    block, blocks = kept, 2 * rows * ACROSS**3 // kept
    half, lanes = width // 2, width // 2
    there, vmem = pl.BlockSpec(memory_space=pltpu.HBM), pl.BlockSpec(memory_space=pltpu.VMEM)
    small = [(16, 128), (ACROSS - 1, 16, 128), (ACROSS, 16, 128), (blocks, block), (N_TILES, 1, 128), (N_TILES, 1, 128)]
    small += [(ACROSS - 1, N_TILES, 1, 128), (ACROSS, 1, N_TILES * slots), (kept, 1), (1, kept)]
    sums = [(2, 4, blocks // 2, block), (2, 10, blocks // 2, block), (2, blocks // 2, block), (kept, width)]
    halves = [(blocks, width, lanes)] * 2 + [(ACROSS, ACROSS, width, lanes)] + [(3, 2, 2, half, lanes)] * 2
    halves += [(ACROSS, half, lanes)] * 2 + [(3, 2, half // 2, lanes)] * 2 + [(ACROSS, rows, width), (3, rows, width)]
    sems = [24, N_TILES, N_TILES, N_TILES, N_TILES, 6, 6, 36, 36, 10, 10, 20, 20, N_TILES, N_TILES, 12, 12, 8, 8, 27, 27]
    return pl.pallas_call(
        step_kernel,
        in_specs=[there] * 6,
        out_specs=[there, vmem],
        out_shape=[
            jax.ShapeDtypeStruct((homes // block, block, width), F32),
            jax.ShapeDtypeStruct((rows, width), F32),
        ],
        scratch_shapes=[
            pltpu.VMEM((rows, width), BF16),
            pltpu.VMEM((1, columns), jnp.int32),
            pltpu.VMEM((1, columns), jnp.int32),
        ]
        + [pltpu.VMEM(shape, jnp.int32) for shape in small]
        + [
            pltpu.VMEM((2, ACROSS, ACROSS, ACROSS, rows, width), BF16),
            pltpu.VMEM((blocks, kept, block), F32),
        ]
        + [pltpu.VMEM(shape, F32) for shape in sums]
        + [pltpu.VMEM((kept, width), BF16), pltpu.VMEM((kept, width), F32)]
        + [pltpu.VMEM((kept, width), BF16), pltpu.VMEM((width, kept), BF16)]
        + [pltpu.VMEM((N_TILES, slots, width), BF16)] * 4
        + [pltpu.VMEM((3, N_TILES, slots, width), BF16)]
        + [pltpu.VMEM(shape, BF16) for shape in halves]
        + [pltpu.SemaphoreType.DMA((n,)) for n in sems],
        compiler_params=pltpu.CompilerParams(
            collective_id=0, has_side_effects=True, vmem_limit_bytes=60 * 2**20
        ),
        name="step",
    )(embeddings, home, row, labels, centres, momentum.reshape(homes // block, block, width))


def finish_kernel(new_ref, centres_ref, emb_ref, momentum_out, centres_out, emb_out):
    momentum = new_ref[...]
    momentum_out[...] = momentum
    centres_out[...] = (centres_ref[...].astype(F32) - learn_rate * momentum).astype(BF16)
    emb_out[...] = emb_ref[...]


def finish(new, centres, emb_grad, rows=512):
    homes, width = centres.shape
    part = pl.BlockSpec((rows, width), lambda i: (i, 0))
    whole = pl.BlockSpec(emb_grad.shape, lambda i: (0, 0))
    return pl.pallas_call(
        finish_kernel,
        grid=(homes // rows,),
        in_specs=[part, part, whole],
        out_specs=[part, part, whole],
        out_shape=[
            jax.ShapeDtypeStruct((homes, width), F32),
            jax.ShapeDtypeStruct((homes, width), BF16),
            jax.ShapeDtypeStruct(emb_grad.shape, F32),
        ],
        compiler_params=pltpu.CompilerParams(vmem_limit_bytes=60 * 2**20),
        name="finish",
    )(new, centres, emb_grad)


def body(embeddings, labels, centres, momentum, sample_home, sample_row):
    columns = sample_row.shape[0]
    new, emb_grad = step(
        embeddings,
        sample_home.reshape(1, columns),
        sample_row.reshape(1, columns),
        labels.reshape(16, 128),
        centres,
        momentum,
    )
    momentum_new, centres_new, emb_grad = finish(new.reshape(centres.shape), centres, emb_grad)
    return (emb_grad, momentum_new, centres_new)


def solution(mesh):
    torus = Mesh(mesh.devices.reshape(mesh.shape["dp"], 4, 4, 2), ("dp", "cls_0", "cls_1", "cls_2"))
    return jax.shard_map(
        body,
        mesh=torus,
        in_specs=(P(DP_CLS, None), P("dp"), P(CLS, None), P(CLS, None), P(CLS, None), P(CLS)),
        out_specs=(P(DP_CLS, None), P(CLS, None), P(CLS, None)),
        check_vma=False,
    )
```

```python
import jax
import jax.numpy as jnp
from jax import lax
from jax.experimental import pallas as pl
from jax.experimental.pallas import tpu as pltpu
from jax.sharding import Mesh
from jax.sharding import PartitionSpec as P

CLS = ("cls_0", "cls_1", "cls_2")
DP_CLS = ("dp", "cls_0", "cls_1", "cls_2")

eps = 1e-06
logit_scale = 64.0
margin = 0.35
momentum_rate = 0.9
learn_rate = 0.1
weight_decay = 0.0005
BF16 = jnp.bfloat16
F32 = jnp.float32


MESH = pl.DeviceIdType.MESH
N_TILES = 32
ACROSS = 4


def where_am_i():
    z, y, x, c = (lax.axis_index(name) for name in DP_CLS)
    return z, y, x, c, y * 8 + x * 2 + c


def ahead(position, k):
    return lax.rem(position + k, ACROSS)


def tile_device(z, t):
    return (z, lax.div(t, 8), lax.rem(lax.div(t, 2), ACROSS), lax.rem(t, 2))


def remote(src, dst, send, recv, device):
    return pltpu.make_async_remote_copy(
        src_ref=src, dst_ref=dst, send_sem=send, recv_sem=recv, device_id=device, device_id_type=MESH
    )


def greet(devices, tiles=None):
    barrier = pltpu.get_barrier_semaphore()
    for device in devices:
        pl.semaphore_signal(barrier, inc=1, device_id=device, device_id_type=MESH)
    count = len(devices)
    if tiles is not None:
        z, me = tiles

        @pl.loop(1, N_TILES)
        def _(k):
            pl.semaphore_signal(
                barrier, inc=1, device_id=tile_device(z, lax.rem(me + k, N_TILES)), device_id_type=MESH
            )

        count += N_TILES - 1
    return barrier, count


def by_lanes(a, b):
    return lax.dot_general(a, b, (((1,), (1,)), ((), ())), preferred_element_type=F32)


def flag(condition):
    return jnp.where(condition, 1.0, 0.0)


def iota(shape, dim):
    return lax.broadcasted_iota(jnp.int32, shape, dim)


def plan_request(home, row, group):
    columns = home.shape[1]
    block = 128
    cuts = [slice(b * block, (b + 1) * block) for b in range(columns // block)]
    at_home = flag(iota((N_TILES, columns), 0) == home)
    upper = flag(iota((block, block), 0) < iota((block, block), 1)).astype(BF16)
    stacked = jnp.concatenate([at_home[:, cut] for cut in cuts], axis=0).astype(BF16)
    within = jnp.dot(stacked, upper, preferred_element_type=F32)
    before = [jnp.zeros((N_TILES, 1), F32)]
    for cut in cuts:
        before.append(before[-1] + jnp.sum(at_home[:, cut], axis=1, keepdims=True))
    count = jnp.broadcast_to(before[-1], (N_TILES, block)).astype(BF16)
    lower = flag(iota((N_TILES, N_TILES), 1) < iota((N_TILES, N_TILES), 0)).astype(BF16)
    offset = jnp.dot(lower, count, preferred_element_type=F32)
    first = ((offset.astype(jnp.int32) + (ACROSS - 1 - group)) >> 2).astype(F32)
    places, starts = [], []
    for b, cut in enumerate(cuts):
        mark = at_home[:, cut]
        rank = within[b * N_TILES : (b + 1) * N_TILES] + before[b] + offset
        places.append(jnp.sum(mark * rank, axis=0, keepdims=True))
        starts.append(jnp.sum(mark * first, axis=0, keepdims=True))
    place = jnp.concatenate(places, axis=1).astype(jnp.int32)
    start = jnp.concatenate(starts, axis=1).astype(jnp.int32)
    mine = (place & 3) == group
    kept = place >> 2
    slot = kept - start
    by_slot = flag(mine & (iota((block, columns), 0) == slot)).astype(BF16)
    digits = [at_home * (row >> 6).astype(F32), at_home * (row & 63).astype(F32)]
    asked = by_lanes(jnp.concatenate(digits, axis=0).astype(BF16), by_slot)
    return (asked[:N_TILES] * 64 + asked[N_TILES:]).astype(jnp.int32), mine, kept, slot


def plan_kept(home, mine, kept, slot, slots):
    columns, block = home.shape[1], 128
    by_kept = flag(mine & (iota((block, columns), 0) == (kept & 127))).astype(BF16)
    lane = iota((1, columns), 1)
    parts = []
    for value in (home, slot, lane >> 6, lane & 63):
        for a in range(ACROSS):
            parts.append(jnp.where((kept >> 7) == a, value.astype(F32), 0.0))
    found = by_lanes(jnp.concatenate(parts, axis=0).astype(BF16), by_kept)
    turned = jnp.concatenate([found, jnp.zeros((block - found.shape[0], block), F32)], axis=0).T
    runs = range(ACROSS)
    slot_row = jnp.concatenate([found[a : a + 1] * slots + found[4 + a : 5 + a] for a in runs], axis=1)
    slot_column = jnp.concatenate([turned[:, a : a + 1] * slots + turned[:, 4 + a : 5 + a] for a in runs], axis=0)
    column = jnp.concatenate([turned[:, 8 + a : 9 + a] * 64 + turned[:, 12 + a : 13 + a] for a in runs], axis=0)
    return slot_row.astype(jnp.int32), slot_column.astype(jnp.int32), column.astype(jnp.int32)


def step_kernel(
    emb_hbm, home_hbm, row_hbm, labels_hbm, centres_hbm, momentum_hbm, momentum_out, emb_out,
    emb, home, row, labels_here, labels_all, labels_at, labels, request, incoming, index_all, index,
    column, slot_row, xall, expo, den, got, inverse, acc, fetched, wunit, scaled, turned, replies, replied, packed, arrived,
    nearby, over, came, mine, first_a, first_b, next_a, next_b, second_a, second_b, last, third,
    local_sem, request_sent, request_came, reply_sent, reply_came, tell_sent, tell_came, phase_sent, phase_came,
    x_sent, x_came, den_sent, den_came, row_sent, row_came, ring_sent, ring_came, over_sent, over_came,
    step_sent, step_came,
):
    z, y, x, c, me = where_am_i()
    other = 1 - c
    partner = (z, y, x, other)
    others = range(ACROSS - 1)
    along_x = [(z, y, ahead(x, k + 1), c) for k in others]
    along_y = [(z, ahead(y, k + 1), x, c) for k in others]
    along_z = [(ahead(z, k + 1), y, x, c) for k in others]
    barrier, count = greet(along_z, (z, me))
    along = {"x": along_x, "y": along_y, "z": along_z}
    pieces = 8
    slots = packed.shape[1]
    block, width = expo.shape[1], expo.shape[2]
    kept = block
    lanes = width // 2

    def local(src, dst, n):
        return pltpu.make_async_copy(src, dst, local_sem.at[n])

    def load_centres(i):
        rows, columns = pl.ds(block * (i // 2), block), pl.ds(lanes * (i % 2), lanes)
        return local(centres_hbm.at[rows, columns], over.at[i], 8 + i)

    small = [
        local(src, dst, n)
        for n, (src, dst) in enumerate(
            ((home_hbm, home), (row_hbm, row), (emb_hbm, emb), (labels_hbm, labels_here))
        )
    ]
    for copy in small:
        copy.start()
    for i in range(2 * pieces):
        load_centres(i).start()
    for copy in small:
        copy.wait()
    xfloat = emb[...].astype(F32)
    row_norm = jnp.sqrt(jnp.sum(xfloat * xfloat, axis=1, keepdims=True) + eps)
    xall[c, z, y, x] = (xfloat / row_norm).astype(BF16)

    def ask(k):
        t = lax.rem(me + k, N_TILES)
        return remote(request.at[t], incoming.at[me], request_sent.at[t], request_came.at[me], tile_device(z, t))

    def asked_by(t):
        return remote(request.at[t], incoming.at[t], request_sent.at[t], request_came.at[t], tile_device(z, t))

    def answer(t):
        return remote(replies.at[t], replied.at[me], reply_sent.at[t], reply_came.at[me], tile_device(z, t))

    def answered(t):
        return remote(replies.at[t], replied.at[t], reply_sent.at[t], reply_came.at[t], tile_device(z, t))

    parts = ((0, 16, "zxy"), (16, 16, "zyx"), (32, 32, "xyz"))
    place = {"z": z, "y": y, "x": x}

    def held(part, phase, position, cut=None):
        first, size, axes = parts[part]
        at = dict(place)
        for n in range(phase):
            at[axes[n]] = pl.ds(0, ACROSS)
        if cut is not None:
            at[axes[0]] = pl.ds(2 * cut, 2)
        at[axes[phase]] = position
        return xall.at[c, at["z"], at["y"], at["x"], pl.ds(first, size)]

    def spread(part, phase, kind):
        axis = parts[part][2][phase]
        position, peers = place[axis], along[axis]
        n = 6 * (3 * part + phase)

        def one(k, ref, peer):
            return remote(ref, ref, phase_sent.at[n + k], phase_came.at[n + k], peers[peer])

        if phase == 0:
            whole = held(part, phase, position)
            return [one(k, whole, k) for k in others]
        here = [held(part, phase, position, cut) for cut in range(2)]
        if kind == 0:
            return [one(0, here[0], 0), one(1, here[1], 2)]
        if kind == 1:
            return [one(2, here[1], 0), one(3, here[0], 2)]
        return [
            one(4, held(part, phase, ahead(position, 3), 0), 0),
            one(5, held(part, phase, ahead(position, 1), 1), 2),
        ]

    flying = []

    def send(copies):
        for copy in copies:
            copy.start()
        flying.extend(copies)

    def land(copies):
        for copy in copies:
            copy.wait_recv()

    def begin(part, phase):
        send(spread(part, phase, 0))
        send(spread(part, phase, 1))

    def forward(part, phase):
        land(spread(part, phase, 0))
        send(spread(part, phase, 2))

    def end(part, phase):
        land(spread(part, phase, 1))
        land(spread(part, phase, 2))

    tell = [
        remote(labels_here, labels_all.at[k], tell_sent.at[k], tell_came.at[k], along_z[k]) for k in others
    ]
    pl.semaphore_wait(barrier, count)
    for part in (2, 0, 1):
        send(spread(part, 0, 0))
    asked, taken, kept_as, slot_at = plan_request(home[...], row[...], z)
    request[...] = asked.reshape(request.shape)
    for part in (2, 0, 1):
        land(spread(part, 0, 0))
        begin(part, 1)

    @pl.loop(1, N_TILES)
    def _(k):
        ask(k).start()

    send(tell)
    incoming[me] = request[me]
    slot_row[...], slot_column, column[...] = plan_kept(home[...], taken, kept_as, slot_at, slots)
    for part in (2, 0, 1):
        forward(part, 1)
    for part in (2, 0, 1):
        end(part, 1)
        begin(part, 2)

    @pl.loop(1, N_TILES)
    def _(k):
        asked_by(lax.rem(me + k, N_TILES)).wait_recv()

    share = [
        remote(incoming, index_all.at[k], tell_sent.at[3 + k], tell_came.at[3 + k], along_z[k]) for k in others
    ]
    send(share)
    for i in range(2 * pieces):
        load_centres(i).wait()
    row_ids = iota((slots, pieces * block), 1)
    for turn, q in enumerate((1, 2, 3, 0)):
        first = ahead(y, q) * 8
        wanted = incoming[pl.ds(first, 8)].reshape(8, 128).T
        pick = jnp.concatenate(
            [flag(row_ids == wanted[:slots, j : j + 1]).astype(BF16) for j in range(8)], axis=0
        )
        found = []
        for h in range(2):
            half_found = jnp.zeros((8 * slots, lanes), F32)
            for r in range(pieces):
                half_found += jnp.dot(
                    pick[:, r * block : (r + 1) * block], over[2 * r + h], preferred_element_type=F32
                )
            found.append(half_found.astype(BF16))
        replies[pl.ds(first, 8)] = jnp.concatenate(found, axis=1).reshape(8, slots, width)
        for j in range(8):
            if q:
                answer(first + j).start()
            else:

                @pl.when(first + j != me)
                def _(t=first + j):
                    answer(t).start()

        if turn == 2:
            for part in (0, 1):
                forward(part, 2)
        if turn == 3:
            forward(2, 2)

    replied[me] = replies[me]
    land(tell + share)
    labels_at[z] = labels_here[...]
    for k in others:
        labels_at[ahead(z, 3 - k)] = labels_all[k]
    rows = emb.shape[0]
    for side in range(2):
        for i in range(pieces):
            runs = [
                labels_at[g, 2 * i + j : 2 * i + j + 1, side * rows : (side + 1) * rows]
                for j in range(2)
                for g in range(ACROSS)
            ]
            labels[side * pieces + i : side * pieces + i + 1] = (
                jnp.concatenate(runs, axis=1) - me * home.shape[1]
            )

    def along_lanes(ref):
        return jnp.concatenate([ref[t][:, :slots] for t in range(N_TILES)], axis=1)

    index[0] = along_lanes(incoming)
    for n, k in ((1, 2), (2, 0), (3, 1)):
        index[n] = along_lanes(index_all.at[k])

    @pl.loop(1, N_TILES)
    def _(k):
        answered(lax.rem(me + k, N_TILES)).wait_recv()

    pick = flag(slot_column == iota((kept, N_TILES * slots), 1)).astype(BF16)
    wfloat = jnp.dot(pick, replied[...].reshape(N_TILES * slots, width), preferred_element_type=F32)
    fetched[...] = wfloat.astype(BF16)
    col_norm = jnp.sqrt(jnp.sum(wfloat * wfloat, axis=1, keepdims=True) + eps)
    wunit[...] = wfloat / col_norm
    scaled[...] = (logit_scale * wunit[...]).astype(BF16)
    turned[...] = wunit[...].T.astype(BF16)

    def swap_part(part, slot):
        first, size, _ = parts[part]
        ref = xall.at[slot, :, :, :, pl.ds(first, size)]
        return remote(ref, ref, x_sent.at[pieces + part], x_came.at[pieces + part], partner)

    def swap_piece(i, slot):
        first, size, _ = parts[2]
        ref = xall.at[slot, :, lax.div(i, 2), pl.ds(2 * lax.rem(i, 2), 2), pl.ds(first, size)]
        return remote(ref, ref, x_sent.at[i], x_came.at[i], partner)

    for part in (0, 1):
        end(part, 2)
        swap_part(part, c).start()
    end(2, 2)

    @pl.loop(0, pieces)
    def _(i):
        swap_piece(i, c).start()

    for part in (0, 1):
        swap_part(part, other).wait_recv()

    def rows_of(side, i):
        y_of, x_of = lax.div(i, 2), 2 * lax.rem(i, 2)
        return jnp.concatenate(
            [xall[side, g, y_of, x_of + j] for j in range(2) for g in range(ACROSS)], axis=0
        )

    def exponents(group, i):
        swap_piece(i, other).wait_recv()
        for side in range(2):
            logit = by_lanes(scaled[...], rows_of(side, i))
            hit = column[...] == labels[pl.ds(side * pieces + i, 1)]
            value = jnp.exp(jnp.where(hit, logit - logit_scale * margin, logit))
            expo[side * pieces + i] = value
            den[group, 0, pl.ds(2 * (i - 4 * group) + side, 1)] = jnp.sum(value, axis=0, keepdims=True)

    stages = ((0, [partner]), (1, along_x), (4, along_y), (7, along_z))

    def stage_copies(group, stage):
        slot, peers = stages[stage]
        return [
            remote(
                den.at[group, stage],
                got.at[group, slot + k],
                den_sent.at[10 * group + slot + k],
                den_came.at[10 * group + slot + k],
                peer,
            )
            for k, peer in enumerate(peers)
        ]

    def stage_start(group, stage):
        for copy in stage_copies(group, stage):
            copy.start()

    def stage_end(group, stage):
        for copy in stage_copies(group, stage):
            copy.wait()
        slot, peers = stages[stage]
        total = den[group, stage]
        for k in range(len(peers)):
            total = total + got[group, slot + k]
        if stage < 3:
            den[group, stage + 1] = total
            stage_start(group, stage + 1)
        else:
            inverse[group] = logit_scale / total

    def gradients(group, i):
        for side in range(2):
            b = side * pieces + i
            hit = column[...] == labels[pl.ds(b, 1)]
            share = expo[b] * inverse[group, pl.ds(2 * (i - 4 * group) + side, 1)]
            grad = jnp.where(hit, share - logit_scale, share).astype(BF16)
            expo[b] = grad.astype(F32)
            acc[...] += jnp.dot(grad, rows_of(side, i), preferred_element_type=F32)

    half = mine.shape[2] // 2
    low, high = pl.ds(0, half), pl.ds(half, half)

    def product(side, i):
        return jnp.dot(turned[...], expo[side * pieces + i].astype(BF16), preferred_element_type=F32)

    def hand_over(i):
        two = pl.ds(2 * i, 2)
        return remote(over.at[two], came.at[two], over_sent.at[i], over_came.at[i], partner)

    def give_over(i):
        part = product(other, i).astype(BF16)
        over[2 * i] = part[:, :lanes]
        over[2 * i + 1] = part[:, lanes:]
        hand_over(i).start()

    def own_part(i):
        part = product(c, i)
        hand_over(i).wait_recv()
        y_of, x_of = lax.div(i, 2), 2 * lax.rem(i, 2)
        mine[y_of, x_of] = (part[:, :lanes] + came[2 * i].astype(F32)).astype(BF16)
        mine[y_of, x_of + 1] = (part[:, lanes:] + came[2 * i + 1].astype(F32)).astype(BF16)

    acc[...] = jnp.zeros_like(acc)

    @pl.loop(0, 4)
    def _(i):
        exponents(0, i)

    stage_start(0, 0)

    @pl.loop(4, pieces)
    def _(i):
        exponents(1, i)

    stage_start(1, 0)
    for n in range(3):
        stage_end(0, n)
        stage_end(1, n)
    stage_end(0, 3)

    @pl.loop(0, 4)
    def _(i):
        gradients(0, i)
        give_over(i)

    stage_end(1, 3)
    @pl.loop(4, pieces)
    def _(i):
        gradients(1, i)

    dwhat = acc[...]
    unit = wunit[...]
    wfloat = fetched[...].astype(F32)
    col_norm = jnp.sqrt(jnp.sum(wfloat * wfloat, axis=1, keepdims=True) + eps)
    dfetched = ((dwhat - unit * jnp.sum(unit * dwhat, axis=1, keepdims=True)) / col_norm).astype(BF16)
    pick = flag(slot_row[...] == iota((N_TILES * slots, kept), 0)).astype(BF16)
    packed[...] = jnp.dot(pick, dfetched, preferred_element_type=F32).astype(BF16).reshape(packed.shape)

    def give(t):
        return remote(packed.at[t], arrived.at[me], row_sent.at[t], row_came.at[me], tile_device(z, t))

    def given(t):
        return remote(packed.at[t], arrived.at[t], row_sent.at[t], row_came.at[t], tile_device(z, t))

    for q in range(ACROSS):
        for j in range(8):
            if q:
                give(8 * ahead(y, q) + j).start()
            else:

                @pl.when(8 * y + j != me)
                def _(t=8 * y + j):
                    give(t).start()

    arrived[me] = packed[me]

    def tiles_of(n):
        return pl.ds(8 * ahead(y, (ACROSS - n) % ACROSS), 8)

    def down(n):
        return remote(
            arrived.at[tiles_of(n)], nearby.at[0, tiles_of(n)], ring_sent.at[n], ring_came.at[n], along_z[2]
        )

    def up(n):
        return remote(
            arrived.at[tiles_of(n)], nearby.at[1, tiles_of(n)], ring_sent.at[4 + n], ring_came.at[4 + n], along_z[0]
        )

    def onward(n):
        source, device = (1, along_z[0]) if n < 2 else (0, along_z[2])
        return remote(
            nearby.at[source, tiles_of(n)],
            nearby.at[2, tiles_of(n)],
            ring_sent.at[8 + n],
            ring_came.at[8 + n],
            device,
        )

    def pass_on(n):
        for j in range(8):
            t = 8 * ahead(y, (ACROSS - n) % ACROSS) + j
            if n:
                given(t).wait_recv()
            else:

                @pl.when(t != me)
                def _(t=t):
                    given(t).wait_recv()

        up(n).start()
        down(n).start()

    pl.loop(4, 8)(give_over)
    pass_on(0)
    pl.loop(0, 8)(own_part)
    pass_on(1)

    def sum_over(n, position, peers, part, inbox):
        up_at, far_at, down_at = (ahead(position, k) for k in (1, 2, 3))

        def hop(k, src, dst, device):
            return remote(src, dst, step_sent.at[n + k], step_came.at[n + k], device)

        early = [
            hop(0, part(far_at, 0), inbox.at[2, 0], peers[0]),
            hop(1, part(far_at, 1), inbox.at[2, 1], peers[2]),
            hop(2, part(up_at, 1), inbox.at[0, 1], peers[0]),
            hop(3, part(down_at, 0), inbox.at[1, 0], peers[2]),
        ]
        late = [hop(4, part(up_at, 0), inbox.at[0, 0], peers[0]), hop(5, part(down_at, 1), inbox.at[1, 1], peers[2])]
        for copy in early:
            copy.start()

        def relay():
            for k, ref in ((0, part(up_at, 0)), (1, part(down_at, 1))):
                early[k].wait_recv()
                ref[...] = (ref[...].astype(F32) + inbox[2, k].astype(F32)).astype(BF16)
                late[k].start()
            flying.extend(early + late)

        return relay, early[2:] + late

    relay_a, rest_a = sum_over(0, x, along_x, lambda p, h: mine.at[pl.ds(2 * h, 2), p, low], first_a)
    relay_b, rest_b = sum_over(6, y, along_y, lambda p, h: mine.at[p, pl.ds(2 * h, 2), high], first_b)

    pass_on(2)
    pass_on(3)

    @pl.loop(0, pieces)
    def _(i):
        hand_over(i).wait_send()

    old = local(momentum_hbm, expo.at[pl.ds(pieces, pieces)], 4)
    old.start()
    for i in range(2 * pieces):
        load_centres(i).start()
    old.wait()
    for i in range(2 * pieces):
        load_centres(i).wait()

    def save(r):
        return local(expo.at[r], momentum_out.at[r], 8 + r)

    def scatter(n, rows_ref, fresh=False, final=False):
        slot_rows = rows_ref.reshape(N_TILES * slots, width)
        wanted = index[n]

        @pl.loop(0, pieces)
        def _(r):
            pick = flag(iota((block, N_TILES * slots), 0) + r * block == wanted).astype(BF16)
            grad = jnp.dot(pick, slot_rows, preferred_element_type=F32)
            if fresh:
                centre = jnp.concatenate([over[2 * r], over[2 * r + 1]], axis=1).astype(F32)
                grad = momentum_rate * expo[pieces + r] + grad + weight_decay * centre
                expo[r] = grad
            else:
                expo[r] = expo[r] + grad
            if final:
                save(r).start()

    for n in range(2):
        up(n).wait_recv()
        onward(n).start()
    scatter(0, arrived[...], fresh=True)
    relay_a()
    relay_b()
    down(2).wait_recv()
    onward(2).start()
    land(rest_a + rest_b)

    @pl.loop(0, ACROSS)
    def _(i):
        h, j = lax.div(i, 2), lax.rem(i, 2)
        total, below = mine[i, x, low].astype(F32), mine[y, i, high].astype(F32)
        for k in range(2):
            total = total + first_a[k, h, j].astype(F32)
            below = below + first_b[k, h, j].astype(F32)
        next_a[i] = total.astype(BF16)
        next_b[i] = below.astype(BF16)

    quarter = half // 2
    relay_a, rest_a = sum_over(12, y, along_y, lambda p, h: next_a.at[p, pl.ds(quarter * h, quarter)], second_a)
    relay_b, rest_b = sum_over(18, x, along_x, lambda p, h: next_b.at[p, pl.ds(quarter * h, quarter)], second_b)
    down(3).wait_recv()
    onward(3).start()
    relay_a()
    relay_b()
    for n in range(2):
        down(n).wait_recv()
    scatter(1, nearby[0])
    for n in range(2, 4):
        up(n).wait_recv()
    scatter(2, nearby[1])
    land(rest_a + rest_b)
    top, bottom = next_a[y].astype(F32), next_b[x].astype(F32)
    for k in range(2):
        top = top + second_a[k].astype(F32).reshape(half, lanes)
        bottom = bottom + second_b[k].astype(F32).reshape(half, lanes)
    last[:, :, :half] = top.T.astype(BF16).reshape(ACROSS, rows, half)
    last[:, :, half:] = bottom.T.astype(BF16).reshape(ACROSS, rows, half)
    three = [
        remote(last.at[ahead(z, k + 1)], third.at[k], step_sent.at[24 + k], step_came.at[24 + k], along_z[k])
        for k in others
    ]
    send(three)
    land([onward(n) for n in range(4)])
    scatter(3, nearby[2], final=True)
    xfloat = emb[...].astype(F32)
    row_norm = jnp.sqrt(jnp.sum(xfloat * xfloat, axis=1, keepdims=True) + eps)
    xunit = xfloat / row_norm
    land(three)
    dunit = last[z].astype(F32)
    for k in others:
        dunit = dunit + third[k].astype(F32)
    emb_out[...] = (dunit - xunit * jnp.sum(xunit * dunit, axis=1, keepdims=True)) / row_norm
    for copy in flying:
        copy.wait_send()
    for n in range(4):
        up(n).wait_send()
        down(n).wait_send()
        onward(n).wait_send()
    for part in (0, 1):
        swap_part(part, c).wait_send()

    @pl.loop(0, pieces)
    def _(i):
        swap_piece(i, c).wait_send()

    @pl.loop(1, N_TILES)
    def _(k):
        ask(k).wait_send()
        answer(lax.rem(me + k, N_TILES)).wait_send()
        give(lax.rem(me + k, N_TILES)).wait_send()

    @pl.loop(0, pieces)
    def _(r):
        save(r).wait()


def step(embeddings, home, row, labels, centres, momentum):
    rows, width = embeddings.shape
    columns = home.shape[1]
    homes = centres.shape[0]
    kept = columns // ACROSS
    slots = 2 * kept // N_TILES
    block, blocks = kept, 2 * rows * ACROSS**3 // kept
    half, lanes = width // 2, width // 2
    there, vmem = pl.BlockSpec(memory_space=pltpu.HBM), pl.BlockSpec(memory_space=pltpu.VMEM)
    small = [(16, 128), (ACROSS - 1, 16, 128), (ACROSS, 16, 128), (blocks, block), (N_TILES, 1, 128), (N_TILES, 1, 128)]
    small += [(ACROSS - 1, N_TILES, 1, 128), (ACROSS, 1, N_TILES * slots), (kept, 1), (1, kept)]
    sums = [(2, 4, blocks // 2, block), (2, 10, blocks // 2, block), (2, blocks // 2, block), (kept, width)]
    halves = [(blocks, width, lanes)] * 2 + [(ACROSS, ACROSS, width, lanes)] + [(3, 2, 2, half, lanes)] * 2
    halves += [(ACROSS, half, lanes)] * 2 + [(3, 2, half // 2, lanes)] * 2 + [(ACROSS, rows, width), (3, rows, width)]
    sems = [24, N_TILES, N_TILES, N_TILES, N_TILES, 6, 6, 54, 54, 10, 10, 20, 20, N_TILES, N_TILES, 12, 12, 8, 8, 27, 27]
    return pl.pallas_call(
        step_kernel,
        in_specs=[there] * 6,
        out_specs=[there, vmem],
        out_shape=[
            jax.ShapeDtypeStruct((homes // block, block, width), F32),
            jax.ShapeDtypeStruct((rows, width), F32),
        ],
        scratch_shapes=[
            pltpu.VMEM((rows, width), BF16),
            pltpu.VMEM((1, columns), jnp.int32),
            pltpu.VMEM((1, columns), jnp.int32),
        ]
        + [pltpu.VMEM(shape, jnp.int32) for shape in small]
        + [
            pltpu.VMEM((2, ACROSS, ACROSS, ACROSS, rows, width), BF16),
            pltpu.VMEM((blocks, kept, block), F32),
        ]
        + [pltpu.VMEM(shape, F32) for shape in sums]
        + [pltpu.VMEM((kept, width), BF16), pltpu.VMEM((kept, width), F32)]
        + [pltpu.VMEM((kept, width), BF16), pltpu.VMEM((width, kept), BF16)]
        + [pltpu.VMEM((N_TILES, slots, width), BF16)] * 4
        + [pltpu.VMEM((3, N_TILES, slots, width), BF16)]
        + [pltpu.VMEM(shape, BF16) for shape in halves]
        + [pltpu.SemaphoreType.DMA((n,)) for n in sems],
        compiler_params=pltpu.CompilerParams(
            collective_id=0, has_side_effects=True, vmem_limit_bytes=60 * 2**20
        ),
        name="step",
    )(embeddings, home, row, labels, centres, momentum.reshape(homes // block, block, width))


def finish_kernel(new_ref, centres_ref, emb_ref, momentum_out, centres_out, emb_out):
    momentum = new_ref[...]
    momentum_out[...] = momentum
    centres_out[...] = (centres_ref[...].astype(F32) - learn_rate * momentum).astype(BF16)
    emb_out[...] = emb_ref[...]


def finish(new, centres, emb_grad, rows=256):
    homes, width = centres.shape
    part = pl.BlockSpec((rows, width), lambda i: (i, 0))
    whole = pl.BlockSpec(emb_grad.shape, lambda i: (0, 0))
    return pl.pallas_call(
        finish_kernel,
        grid=(homes // rows,),
        in_specs=[part, part, whole],
        out_specs=[part, part, whole],
        out_shape=[
            jax.ShapeDtypeStruct((homes, width), F32),
            jax.ShapeDtypeStruct((homes, width), BF16),
            jax.ShapeDtypeStruct(emb_grad.shape, F32),
        ],
        compiler_params=pltpu.CompilerParams(vmem_limit_bytes=60 * 2**20),
        name="finish",
    )(new, centres, emb_grad)


def body(embeddings, labels, centres, momentum, sample_home, sample_row):
    columns = sample_row.shape[0]
    new, emb_grad = step(
        embeddings,
        sample_home.reshape(1, columns),
        sample_row.reshape(1, columns),
        labels.reshape(16, 128),
        centres,
        momentum,
    )
    momentum_new, centres_new, emb_grad = finish(new.reshape(centres.shape), centres, emb_grad)
    return (emb_grad, momentum_new, centres_new)


def solution(mesh):
    torus = Mesh(mesh.devices.reshape(mesh.shape["dp"], 4, 4, 2), ("dp", "cls_0", "cls_1", "cls_2"))
    return jax.shard_map(
        body,
        mesh=torus,
        in_specs=(P(DP_CLS, None), P("dp"), P(CLS, None), P(CLS, None), P(CLS, None), P(CLS)),
        out_specs=(P(DP_CLS, None), P(CLS, None), P(CLS, None)),
        check_vma=False,
    )
```

```python
import jax
import jax.numpy as jnp
from jax import lax
from jax.experimental import pallas as pl
from jax.experimental.pallas import tpu as pltpu
from jax.sharding import Mesh
from jax.sharding import PartitionSpec as P

CLS = ("cls_0", "cls_1", "cls_2")
DP_CLS = ("dp", "cls_0", "cls_1", "cls_2")

eps = 1e-06
logit_scale = 64.0
margin = 0.35
momentum_rate = 0.9
learn_rate = 0.1
weight_decay = 0.0005
BF16 = jnp.bfloat16
F32 = jnp.float32


MESH = pl.DeviceIdType.MESH
N_TILES = 32
ACROSS = 4


def where_am_i():
    z, y, x, c = (lax.axis_index(name) for name in DP_CLS)
    return z, y, x, c, y * 8 + x * 2 + c


def ahead(position, k):
    return lax.rem(position + k, ACROSS)


def tile_device(z, t):
    return (z, lax.div(t, 8), lax.rem(lax.div(t, 2), ACROSS), lax.rem(t, 2))


def remote(src, dst, send, recv, device):
    return pltpu.make_async_remote_copy(
        src_ref=src, dst_ref=dst, send_sem=send, recv_sem=recv, device_id=device, device_id_type=MESH
    )


def greet(devices, tiles=None):
    barrier = pltpu.get_barrier_semaphore()
    for device in devices:
        pl.semaphore_signal(barrier, inc=1, device_id=device, device_id_type=MESH)
    count = len(devices)
    if tiles is not None:
        z, me = tiles

        @pl.loop(1, N_TILES)
        def _(k):
            pl.semaphore_signal(
                barrier, inc=1, device_id=tile_device(z, lax.rem(me + k, N_TILES)), device_id_type=MESH
            )

        count += N_TILES - 1
    return barrier, count


def by_lanes(a, b):
    return lax.dot_general(a, b, (((1,), (1,)), ((), ())), preferred_element_type=F32)


def flag(condition):
    return jnp.where(condition, 1.0, 0.0)


def iota(shape, dim):
    return lax.broadcasted_iota(jnp.int32, shape, dim)


def plan_request(home, row, group):
    columns = home.shape[1]
    block = 128
    cuts = [slice(b * block, (b + 1) * block) for b in range(columns // block)]
    at_home = flag(iota((N_TILES, columns), 0) == home)
    upper = flag(iota((block, block), 0) < iota((block, block), 1)).astype(BF16)
    stacked = jnp.concatenate([at_home[:, cut] for cut in cuts], axis=0).astype(BF16)
    within = jnp.dot(stacked, upper, preferred_element_type=F32)
    before = [jnp.zeros((N_TILES, 1), F32)]
    for cut in cuts:
        before.append(before[-1] + jnp.sum(at_home[:, cut], axis=1, keepdims=True))
    count = jnp.broadcast_to(before[-1], (N_TILES, block)).astype(BF16)
    lower = flag(iota((N_TILES, N_TILES), 1) < iota((N_TILES, N_TILES), 0)).astype(BF16)
    offset = jnp.dot(lower, count, preferred_element_type=F32)
    first = ((offset.astype(jnp.int32) + (ACROSS - 1 - group)) >> 2).astype(F32)
    places, starts = [], []
    for b, cut in enumerate(cuts):
        mark = at_home[:, cut]
        rank = within[b * N_TILES : (b + 1) * N_TILES] + before[b] + offset
        places.append(jnp.sum(mark * rank, axis=0, keepdims=True))
        starts.append(jnp.sum(mark * first, axis=0, keepdims=True))
    place = jnp.concatenate(places, axis=1).astype(jnp.int32)
    start = jnp.concatenate(starts, axis=1).astype(jnp.int32)
    mine = (place & 3) == group
    kept = place >> 2
    slot = kept - start
    by_slot = flag(mine & (iota((block, columns), 0) == slot)).astype(BF16)
    digits = [at_home * (row >> 6).astype(F32), at_home * (row & 63).astype(F32)]
    asked = by_lanes(jnp.concatenate(digits, axis=0).astype(BF16), by_slot)
    return (asked[:N_TILES] * 64 + asked[N_TILES:]).astype(jnp.int32), mine, kept, slot


def plan_kept(home, mine, kept, slot, slots):
    columns, block = home.shape[1], 128
    by_kept = flag(mine & (iota((block, columns), 0) == (kept & 127))).astype(BF16)
    lane = iota((1, columns), 1)
    parts = []
    for value in (home, slot, lane >> 6, lane & 63):
        for a in range(ACROSS):
            parts.append(jnp.where((kept >> 7) == a, value.astype(F32), 0.0))
    found = by_lanes(jnp.concatenate(parts, axis=0).astype(BF16), by_kept)
    turned = jnp.concatenate([found, jnp.zeros((block - found.shape[0], block), F32)], axis=0).T
    runs = range(ACROSS)
    slot_row = jnp.concatenate([found[a : a + 1] * slots + found[4 + a : 5 + a] for a in runs], axis=1)
    slot_column = jnp.concatenate([turned[:, a : a + 1] * slots + turned[:, 4 + a : 5 + a] for a in runs], axis=0)
    column = jnp.concatenate([turned[:, 8 + a : 9 + a] * 64 + turned[:, 12 + a : 13 + a] for a in runs], axis=0)
    return slot_row.astype(jnp.int32), slot_column.astype(jnp.int32), column.astype(jnp.int32)


def step_kernel(
    emb_hbm, home_hbm, row_hbm, labels_hbm, centres_hbm, momentum_hbm, momentum_out, emb_out,
    emb, home, row, labels_here, labels_all, labels_at, labels, request, incoming, index_all, index,
    column, slot_row, xall, expo, den, got, inverse, acc, fetched, wunit, scaled, turned, replies, replied, packed, arrived,
    nearby, over, came, mine, first_a, first_b, next_a, next_b, second_a, second_b, last, third,
    local_sem, request_sent, request_came, reply_sent, reply_came, tell_sent, tell_came, phase_sent, phase_came,
    x_sent, x_came, den_sent, den_came, row_sent, row_came, ring_sent, ring_came, over_sent, over_came,
    step_sent, step_came,
):
    z, y, x, c, me = where_am_i()
    other = 1 - c
    partner = (z, y, x, other)
    others = range(ACROSS - 1)
    along_x = [(z, y, ahead(x, k + 1), c) for k in others]
    along_y = [(z, ahead(y, k + 1), x, c) for k in others]
    along_z = [(ahead(z, k + 1), y, x, c) for k in others]
    barrier, count = greet(along_z, (z, me))
    along = {"x": along_x, "y": along_y, "z": along_z}
    pieces = 8
    slots = packed.shape[1]
    block, width = expo.shape[1], expo.shape[2]
    kept = block
    lanes = width // 2

    def local(src, dst, n):
        return pltpu.make_async_copy(src, dst, local_sem.at[n])

    def load_centres(i):
        rows, columns = pl.ds(block * (i // 2), block), pl.ds(lanes * (i % 2), lanes)
        return local(centres_hbm.at[rows, columns], over.at[i], 8 + i)

    small = [
        local(src, dst, n)
        for n, (src, dst) in enumerate(
            ((home_hbm, home), (row_hbm, row), (emb_hbm, emb), (labels_hbm, labels_here))
        )
    ]
    for copy in small:
        copy.start()
    for i in range(2 * pieces):
        load_centres(i).start()
    for copy in small:
        copy.wait()
    xfloat = emb[...].astype(F32)
    row_norm = jnp.sqrt(jnp.sum(xfloat * xfloat, axis=1, keepdims=True) + eps)
    xall[c, z, y, x] = (xfloat / row_norm).astype(BF16)

    def ask(k):
        t = lax.rem(me + k, N_TILES)
        return remote(request.at[t], incoming.at[me], request_sent.at[t], request_came.at[me], tile_device(z, t))

    def asked_by(t):
        return remote(request.at[t], incoming.at[t], request_sent.at[t], request_came.at[t], tile_device(z, t))

    def answer(t):
        return remote(replies.at[t], replied.at[me], reply_sent.at[t], reply_came.at[me], tile_device(z, t))

    def answered(t):
        return remote(replies.at[t], replied.at[t], reply_sent.at[t], reply_came.at[t], tile_device(z, t))

    parts = ((0, 16, "zxy"), (16, 16, "zyx"), (32, 32, "xyz"))
    place = {"z": z, "y": y, "x": x}

    def held(part, phase, position, cut=None):
        first, size, axes = parts[part]
        at = dict(place)
        for n in range(phase):
            at[axes[n]] = pl.ds(0, ACROSS)
        if cut is not None:
            at[axes[0]] = pl.ds(2 * cut, 2)
        at[axes[phase]] = position
        return xall.at[c, at["z"], at["y"], at["x"], pl.ds(first, size)]

    def spread(part, phase, kind):
        axis = parts[part][2][phase]
        position, peers = place[axis], along[axis]
        n = 6 * (3 * part + phase)

        def one(k, ref, peer):
            return remote(ref, ref, phase_sent.at[n + k], phase_came.at[n + k], peers[peer])

        if phase == 0:
            whole = held(part, phase, position)
            return [one(k, whole, k) for k in others]
        here = [held(part, phase, position, cut) for cut in range(2)]
        if kind == 0:
            return [one(0, here[0], 0), one(1, here[1], 2)]
        if kind == 1:
            return [one(2, here[1], 0), one(3, here[0], 2)]
        return [
            one(4, held(part, phase, ahead(position, 3), 0), 0),
            one(5, held(part, phase, ahead(position, 1), 1), 2),
        ]

    flying = []

    def send(copies):
        for copy in copies:
            copy.start()
        flying.extend(copies)

    def land(copies):
        for copy in copies:
            copy.wait_recv()

    def begin(part, phase):
        send(spread(part, phase, 0))
        send(spread(part, phase, 1))

    def forward(part, phase):
        land(spread(part, phase, 0))
        send(spread(part, phase, 2))

    def end(part, phase):
        land(spread(part, phase, 1))
        land(spread(part, phase, 2))

    tell = [
        remote(labels_here, labels_all.at[k], tell_sent.at[k], tell_came.at[k], along_z[k]) for k in others
    ]
    pl.semaphore_wait(barrier, count)
    for part in (2, 0, 1):
        send(spread(part, 0, 0))
    asked, taken, kept_as, slot_at = plan_request(home[...], row[...], z)
    request[...] = asked.reshape(request.shape)
    for part in (2, 0, 1):
        land(spread(part, 0, 0))
        begin(part, 1)

    @pl.loop(1, N_TILES)
    def _(k):
        ask(k).start()

    send(tell)
    incoming[me] = request[me]
    slot_row[...], slot_column, column[...] = plan_kept(home[...], taken, kept_as, slot_at, slots)
    for part in (2, 0, 1):
        forward(part, 1)
    for part in (2, 0, 1):
        end(part, 1)
        begin(part, 2)

    @pl.loop(1, N_TILES)
    def _(k):
        asked_by(lax.rem(me + k, N_TILES)).wait_recv()

    share = [
        remote(incoming, index_all.at[k], tell_sent.at[3 + k], tell_came.at[3 + k], along_z[k]) for k in others
    ]
    send(share)
    for i in range(2 * pieces):
        load_centres(i).wait()
    row_ids = iota((slots, pieces * block), 1)
    for turn, q in enumerate((1, 2, 3, 0)):
        first = ahead(y, q) * 8
        wanted = incoming[pl.ds(first, 8)].reshape(8, 128).T
        pick = jnp.concatenate(
            [flag(row_ids == wanted[:slots, j : j + 1]).astype(BF16) for j in range(8)], axis=0
        )
        found = []
        for h in range(2):
            half_found = jnp.zeros((8 * slots, lanes), F32)
            for r in range(pieces):
                half_found += jnp.dot(
                    pick[:, r * block : (r + 1) * block], over[2 * r + h], preferred_element_type=F32
                )
            found.append(half_found.astype(BF16))
        replies[pl.ds(first, 8)] = jnp.concatenate(found, axis=1).reshape(8, slots, width)
        for j in range(8):
            if q:
                answer(first + j).start()
            else:

                @pl.when(first + j != me)
                def _(t=first + j):
                    answer(t).start()

        if turn == 2:
            for part in (0, 1):
                forward(part, 2)
        if turn == 3:
            forward(2, 2)

    replied[me] = replies[me]
    land(tell + share)
    labels_at[z] = labels_here[...]
    for k in others:
        labels_at[ahead(z, 3 - k)] = labels_all[k]
    rows = emb.shape[0]
    for side in range(2):
        for i in range(pieces):
            runs = [
                labels_at[g, 2 * i + j : 2 * i + j + 1, side * rows : (side + 1) * rows]
                for j in range(2)
                for g in range(ACROSS)
            ]
            labels[side * pieces + i : side * pieces + i + 1] = (
                jnp.concatenate(runs, axis=1) - me * home.shape[1]
            )

    def along_lanes(ref):
        return jnp.concatenate([ref[t][:, :slots] for t in range(N_TILES)], axis=1)

    index[0] = along_lanes(incoming)
    for n, k in ((1, 2), (2, 0), (3, 1)):
        index[n] = along_lanes(index_all.at[k])

    @pl.loop(1, N_TILES)
    def _(k):
        answered(lax.rem(me + k, N_TILES)).wait_recv()

    pick = flag(slot_column == iota((kept, N_TILES * slots), 1)).astype(BF16)
    wfloat = jnp.dot(pick, replied[...].reshape(N_TILES * slots, width), preferred_element_type=F32)
    fetched[...] = wfloat.astype(BF16)
    col_norm = jnp.sqrt(jnp.sum(wfloat * wfloat, axis=1, keepdims=True) + eps)
    wunit[...] = wfloat / col_norm
    scaled[...] = (logit_scale * wunit[...]).astype(BF16)
    turned[...] = wunit[...].T.astype(BF16)

    def swap_part(part, slot):
        first, size, _ = parts[part]
        ref = xall.at[slot, :, :, :, pl.ds(first, size)]
        return remote(ref, ref, x_sent.at[pieces + part], x_came.at[pieces + part], partner)

    def swap_piece(i, slot):
        first, size, _ = parts[2]
        ref = xall.at[slot, :, lax.div(i, 2), pl.ds(2 * lax.rem(i, 2), 2), pl.ds(first, size)]
        return remote(ref, ref, x_sent.at[i], x_came.at[i], partner)

    for part in (0, 1):
        end(part, 2)
        swap_part(part, c).start()
    end(2, 2)

    @pl.loop(0, pieces)
    def _(i):
        swap_piece(i, c).start()

    for part in (0, 1):
        swap_part(part, other).wait_recv()

    def rows_of(side, i):
        y_of, x_of = lax.div(i, 2), 2 * lax.rem(i, 2)
        return jnp.concatenate(
            [xall[side, g, y_of, x_of + j] for j in range(2) for g in range(ACROSS)], axis=0
        )

    def exponents(group, i):
        swap_piece(i, other).wait_recv()
        for side in range(2):
            logit = by_lanes(scaled[...], rows_of(side, i))
            hit = column[...] == labels[pl.ds(side * pieces + i, 1)]
            value = jnp.exp(jnp.where(hit, logit - logit_scale * margin, logit))
            expo[side * pieces + i] = value
            den[group, 0, pl.ds(2 * (i - 4 * group) + side, 1)] = jnp.sum(value, axis=0, keepdims=True)

    stages = ((0, [partner]), (1, along_x), (4, along_y), (7, along_z))

    def stage_copies(group, stage):
        slot, peers = stages[stage]
        return [
            remote(
                den.at[group, stage],
                got.at[group, slot + k],
                den_sent.at[10 * group + slot + k],
                den_came.at[10 * group + slot + k],
                peer,
            )
            for k, peer in enumerate(peers)
        ]

    def swap_inverse(group):
        ref = inverse.at[group]
        return remote(ref, ref, den_sent.at[20 + group], den_came.at[20 + group], partner)

    def sum_denominators():
        stage_copies(other, 0)[0].start()
        stage_copies(c, 0)[0].wait_recv()
        den[c, 1] = den[c, 0] + got[c, 0]
        for stage in range(1, 4):
            copies = stage_copies(c, stage)
            for copy in copies:
                copy.start()
            for copy in copies:
                copy.wait_recv()
            total = den[c, stage]
            for k in range(len(copies)):
                total = total + got[c, stages[stage][0] + k]
            if stage < 3:
                den[c, stage + 1] = total
            else:
                inverse[c] = logit_scale / total
        swap_inverse(c).start()
        swap_inverse(other).wait_recv()

    def gradients(group, i):
        for side in range(2):
            b = side * pieces + i
            hit = column[...] == labels[pl.ds(b, 1)]
            share = expo[b] * inverse[group, pl.ds(2 * (i - 4 * group) + side, 1)]
            grad = jnp.where(hit, share - logit_scale, share).astype(BF16)
            expo[b] = grad.astype(F32)
            acc[...] += jnp.dot(grad, rows_of(side, i), preferred_element_type=F32)

    half = mine.shape[2] // 2
    low, high = pl.ds(0, half), pl.ds(half, half)

    def product(side, i):
        return jnp.dot(turned[...], expo[side * pieces + i].astype(BF16), preferred_element_type=F32)

    def hand_over(i):
        two = pl.ds(2 * i, 2)
        return remote(over.at[two], came.at[two], over_sent.at[i], over_came.at[i], partner)

    def give_over(i):
        part = product(other, i).astype(BF16)
        over[2 * i] = part[:, :lanes]
        over[2 * i + 1] = part[:, lanes:]
        hand_over(i).start()

    def own_part(i):
        part = product(c, i)
        hand_over(i).wait_recv()
        y_of, x_of = lax.div(i, 2), 2 * lax.rem(i, 2)
        mine[y_of, x_of] = (part[:, :lanes] + came[2 * i].astype(F32)).astype(BF16)
        mine[y_of, x_of + 1] = (part[:, lanes:] + came[2 * i + 1].astype(F32)).astype(BF16)

    acc[...] = jnp.zeros_like(acc)

    @pl.loop(0, 4)
    def _(i):
        exponents(0, i)

    @pl.loop(4, pieces)
    def _(i):
        exponents(1, i)

    sum_denominators()

    @pl.loop(0, 4)
    def _(i):
        gradients(0, i)
        give_over(i)

    @pl.loop(4, pieces)
    def _(i):
        gradients(1, i)

    dwhat = acc[...]
    unit = wunit[...]
    wfloat = fetched[...].astype(F32)
    col_norm = jnp.sqrt(jnp.sum(wfloat * wfloat, axis=1, keepdims=True) + eps)
    dfetched = ((dwhat - unit * jnp.sum(unit * dwhat, axis=1, keepdims=True)) / col_norm).astype(BF16)
    pick = flag(slot_row[...] == iota((N_TILES * slots, kept), 0)).astype(BF16)
    packed[...] = jnp.dot(pick, dfetched, preferred_element_type=F32).astype(BF16).reshape(packed.shape)

    def give(t):
        return remote(packed.at[t], arrived.at[me], row_sent.at[t], row_came.at[me], tile_device(z, t))

    def given(t):
        return remote(packed.at[t], arrived.at[t], row_sent.at[t], row_came.at[t], tile_device(z, t))

    for q in range(ACROSS):
        for j in range(8):
            if q:
                give(8 * ahead(y, q) + j).start()
            else:

                @pl.when(8 * y + j != me)
                def _(t=8 * y + j):
                    give(t).start()

    arrived[me] = packed[me]

    def tiles_of(n):
        return pl.ds(8 * ahead(y, (ACROSS - n) % ACROSS), 8)

    def down(n):
        return remote(
            arrived.at[tiles_of(n)], nearby.at[0, tiles_of(n)], ring_sent.at[n], ring_came.at[n], along_z[2]
        )

    def up(n):
        return remote(
            arrived.at[tiles_of(n)], nearby.at[1, tiles_of(n)], ring_sent.at[4 + n], ring_came.at[4 + n], along_z[0]
        )

    def onward(n):
        source, device = (1, along_z[0]) if n < 2 else (0, along_z[2])
        return remote(
            nearby.at[source, tiles_of(n)],
            nearby.at[2, tiles_of(n)],
            ring_sent.at[8 + n],
            ring_came.at[8 + n],
            device,
        )

    def pass_on(n):
        for j in range(8):
            t = 8 * ahead(y, (ACROSS - n) % ACROSS) + j
            if n:
                given(t).wait_recv()
            else:

                @pl.when(t != me)
                def _(t=t):
                    given(t).wait_recv()

        up(n).start()
        down(n).start()

    pl.loop(4, 8)(give_over)
    pass_on(0)
    pl.loop(0, 8)(own_part)
    pass_on(1)

    def sum_over(n, position, peers, part, inbox):
        up_at, far_at, down_at = (ahead(position, k) for k in (1, 2, 3))

        def hop(k, src, dst, device):
            return remote(src, dst, step_sent.at[n + k], step_came.at[n + k], device)

        early = [
            hop(0, part(far_at, 0), inbox.at[2, 0], peers[0]),
            hop(1, part(far_at, 1), inbox.at[2, 1], peers[2]),
            hop(2, part(up_at, 1), inbox.at[0, 1], peers[0]),
            hop(3, part(down_at, 0), inbox.at[1, 0], peers[2]),
        ]
        late = [hop(4, part(up_at, 0), inbox.at[0, 0], peers[0]), hop(5, part(down_at, 1), inbox.at[1, 1], peers[2])]
        for copy in early:
            copy.start()

        def relay():
            for k, ref in ((0, part(up_at, 0)), (1, part(down_at, 1))):
                early[k].wait_recv()
                ref[...] = (ref[...].astype(F32) + inbox[2, k].astype(F32)).astype(BF16)
                late[k].start()
            flying.extend(early + late)

        return relay, early[2:] + late

    relay_a, rest_a = sum_over(0, x, along_x, lambda p, h: mine.at[pl.ds(2 * h, 2), p, low], first_a)
    relay_b, rest_b = sum_over(6, y, along_y, lambda p, h: mine.at[p, pl.ds(2 * h, 2), high], first_b)

    pass_on(2)
    pass_on(3)

    @pl.loop(0, pieces)
    def _(i):
        hand_over(i).wait_send()

    old = local(momentum_hbm, expo.at[pl.ds(pieces, pieces)], 4)
    old.start()
    for i in range(2 * pieces):
        load_centres(i).start()
    old.wait()
    for i in range(2 * pieces):
        load_centres(i).wait()

    def save(r):
        return local(expo.at[r], momentum_out.at[r], 8 + r)

    def scatter(n, rows_ref, fresh=False, final=False):
        slot_rows = rows_ref.reshape(N_TILES * slots, width)
        wanted = index[n]

        @pl.loop(0, pieces)
        def _(r):
            pick = flag(iota((block, N_TILES * slots), 0) + r * block == wanted).astype(BF16)
            grad = jnp.dot(pick, slot_rows, preferred_element_type=F32)
            if fresh:
                centre = jnp.concatenate([over[2 * r], over[2 * r + 1]], axis=1).astype(F32)
                grad = momentum_rate * expo[pieces + r] + grad + weight_decay * centre
                expo[r] = grad
            else:
                expo[r] = expo[r] + grad
            if final:
                save(r).start()

    for n in range(2):
        up(n).wait_recv()
        onward(n).start()
    scatter(0, arrived[...], fresh=True)
    relay_a()
    relay_b()
    down(2).wait_recv()
    onward(2).start()
    land(rest_a + rest_b)

    @pl.loop(0, ACROSS)
    def _(i):
        h, j = lax.div(i, 2), lax.rem(i, 2)
        total, below = mine[i, x, low].astype(F32), mine[y, i, high].astype(F32)
        for k in range(2):
            total = total + first_a[k, h, j].astype(F32)
            below = below + first_b[k, h, j].astype(F32)
        next_a[i] = total.astype(BF16)
        next_b[i] = below.astype(BF16)

    quarter = half // 2
    relay_a, rest_a = sum_over(12, y, along_y, lambda p, h: next_a.at[p, pl.ds(quarter * h, quarter)], second_a)
    relay_b, rest_b = sum_over(18, x, along_x, lambda p, h: next_b.at[p, pl.ds(quarter * h, quarter)], second_b)
    down(3).wait_recv()
    onward(3).start()
    relay_a()
    relay_b()
    for n in range(2):
        down(n).wait_recv()
    scatter(1, nearby[0])
    for n in range(2, 4):
        up(n).wait_recv()
    scatter(2, nearby[1])
    land(rest_a + rest_b)
    top, bottom = next_a[y].astype(F32), next_b[x].astype(F32)
    for k in range(2):
        top = top + second_a[k].astype(F32).reshape(half, lanes)
        bottom = bottom + second_b[k].astype(F32).reshape(half, lanes)
    last[:, :, :half] = top.T.astype(BF16).reshape(ACROSS, rows, half)
    last[:, :, half:] = bottom.T.astype(BF16).reshape(ACROSS, rows, half)
    three = [
        remote(last.at[ahead(z, k + 1)], third.at[k], step_sent.at[24 + k], step_came.at[24 + k], along_z[k])
        for k in others
    ]
    send(three)
    land([onward(n) for n in range(4)])
    scatter(3, nearby[2], final=True)
    xfloat = emb[...].astype(F32)
    row_norm = jnp.sqrt(jnp.sum(xfloat * xfloat, axis=1, keepdims=True) + eps)
    xunit = xfloat / row_norm
    land(three)
    dunit = last[z].astype(F32)
    for k in others:
        dunit = dunit + third[k].astype(F32)
    emb_out[...] = (dunit - xunit * jnp.sum(xunit * dunit, axis=1, keepdims=True)) / row_norm
    for copy in flying:
        copy.wait_send()
    for n in range(4):
        up(n).wait_send()
        down(n).wait_send()
        onward(n).wait_send()
    for part in (0, 1):
        swap_part(part, c).wait_send()
    stage_copies(other, 0)[0].wait_send()
    for stage in range(1, 4):
        for copy in stage_copies(c, stage):
            copy.wait_send()
    swap_inverse(c).wait_send()

    @pl.loop(0, pieces)
    def _(i):
        swap_piece(i, c).wait_send()

    @pl.loop(1, N_TILES)
    def _(k):
        ask(k).wait_send()
        answer(lax.rem(me + k, N_TILES)).wait_send()
        give(lax.rem(me + k, N_TILES)).wait_send()

    @pl.loop(0, pieces)
    def _(r):
        save(r).wait()


def step(embeddings, home, row, labels, centres, momentum):
    rows, width = embeddings.shape
    columns = home.shape[1]
    homes = centres.shape[0]
    kept = columns // ACROSS
    slots = 2 * kept // N_TILES
    block, blocks = kept, 2 * rows * ACROSS**3 // kept
    half, lanes = width // 2, width // 2
    there, vmem = pl.BlockSpec(memory_space=pltpu.HBM), pl.BlockSpec(memory_space=pltpu.VMEM)
    small = [(16, 128), (ACROSS - 1, 16, 128), (ACROSS, 16, 128), (blocks, block), (N_TILES, 1, 128), (N_TILES, 1, 128)]
    small += [(ACROSS - 1, N_TILES, 1, 128), (ACROSS, 1, N_TILES * slots), (kept, 1), (1, kept)]
    sums = [(2, 4, blocks // 2, block), (2, 10, blocks // 2, block), (2, blocks // 2, block), (kept, width)]
    halves = [(blocks, width, lanes)] * 2 + [(ACROSS, ACROSS, width, lanes)] + [(3, 2, 2, half, lanes)] * 2
    halves += [(ACROSS, half, lanes)] * 2 + [(3, 2, half // 2, lanes)] * 2 + [(ACROSS, rows, width), (3, rows, width)]
    sems = [24, N_TILES, N_TILES, N_TILES, N_TILES, 6, 6, 54, 54, 11, 11, 22, 22, N_TILES, N_TILES, 12, 12, 8, 8, 27, 27]
    return pl.pallas_call(
        step_kernel,
        in_specs=[there] * 6,
        out_specs=[there, vmem],
        out_shape=[
            jax.ShapeDtypeStruct((homes // block, block, width), F32),
            jax.ShapeDtypeStruct((rows, width), F32),
        ],
        scratch_shapes=[
            pltpu.VMEM((rows, width), BF16),
            pltpu.VMEM((1, columns), jnp.int32),
            pltpu.VMEM((1, columns), jnp.int32),
        ]
        + [pltpu.VMEM(shape, jnp.int32) for shape in small]
        + [
            pltpu.VMEM((2, ACROSS, ACROSS, ACROSS, rows, width), BF16),
            pltpu.VMEM((blocks, kept, block), F32),
        ]
        + [pltpu.VMEM(shape, F32) for shape in sums]
        + [pltpu.VMEM((kept, width), BF16), pltpu.VMEM((kept, width), F32)]
        + [pltpu.VMEM((kept, width), BF16), pltpu.VMEM((width, kept), BF16)]
        + [pltpu.VMEM((N_TILES, slots, width), BF16)] * 4
        + [pltpu.VMEM((3, N_TILES, slots, width), BF16)]
        + [pltpu.VMEM(shape, BF16) for shape in halves]
        + [pltpu.SemaphoreType.DMA((n,)) for n in sems],
        compiler_params=pltpu.CompilerParams(
            collective_id=0, has_side_effects=True, vmem_limit_bytes=60 * 2**20
        ),
        name="step",
    )(embeddings, home, row, labels, centres, momentum.reshape(homes // block, block, width))


def finish_kernel(new_ref, centres_ref, emb_ref, momentum_out, centres_out, emb_out):
    momentum = new_ref[...]
    momentum_out[...] = momentum
    centres_out[...] = (centres_ref[...].astype(F32) - learn_rate * momentum).astype(BF16)
    emb_out[...] = emb_ref[...]


def finish(new, centres, emb_grad, rows=1024):
    homes, width = centres.shape
    part = pl.BlockSpec((rows, width), lambda i: (i, 0))
    whole = pl.BlockSpec(emb_grad.shape, lambda i: (0, 0))
    return pl.pallas_call(
        finish_kernel,
        grid=(homes // rows,),
        in_specs=[part, part, whole],
        out_specs=[part, part, whole],
        out_shape=[
            jax.ShapeDtypeStruct((homes, width), F32),
            jax.ShapeDtypeStruct((homes, width), BF16),
            jax.ShapeDtypeStruct(emb_grad.shape, F32),
        ],
        compiler_params=pltpu.CompilerParams(vmem_limit_bytes=60 * 2**20),
        name="finish",
    )(new, centres, emb_grad)


def body(embeddings, labels, centres, momentum, sample_home, sample_row):
    columns = sample_row.shape[0]
    new, emb_grad = step(
        embeddings,
        sample_home.reshape(1, columns),
        sample_row.reshape(1, columns),
        labels.reshape(16, 128),
        centres,
        momentum,
    )
    momentum_new, centres_new, emb_grad = finish(new.reshape(centres.shape), centres, emb_grad)
    return (emb_grad, momentum_new, centres_new)


def solution(mesh):
    torus = Mesh(mesh.devices.reshape(mesh.shape["dp"], 4, 4, 2), ("dp", "cls_0", "cls_1", "cls_2"))
    return jax.shard_map(
        body,
        mesh=torus,
        in_specs=(P(DP_CLS, None), P("dp"), P(CLS, None), P(CLS, None), P(CLS, None), P(CLS)),
        out_specs=(P(DP_CLS, None), P(CLS, None), P(CLS, None)),
        check_vma=False,
    )
```
